128 devices in a mesh: tile: 16 (over x, y_hi, core), gz: 8 (over z, y_lo).
Axes of the slice: x: 4, y: 4 (y_hi: 2, y_lo: 2; y = y_hi * 2 + y_lo), z: 4, core: 2. Of those that a mesh axis runs over, the one named last changes fastest.
Arguments:
- trans_x: float32 [256, 128, 512], P('tile', 'gz'), may hold values from 3 to 10
- trans_y: float32 [256, 128, 512], P('tile', 'gz'), may hold values from 0.5 to 2
- trans_z: float32 [256, 128, 512], P('tile', 'gz'), may hold values from 0.1 to 0.3
- accumulation: float32 [256, 128, 512], P('tile', 'gz'), may hold values from 0.02 to 0.2
- source: float32 [256, 128, 512], P('tile', 'gz'), may hold values from -6 to 6
- well_cell: int32 [256, 8], P('tile', 'gz'), may hold values from 0 to 131071
- well_rate: float32 [256, 8], P('tile', 'gz'), may hold values from -48 to 48
Outputs:
- basis: float32 [8, 256, 128, 512], P(None, 'tile', 'gz')
- pressure: float32 [256, 128, 512], P('tile', 'gz')
- residual: float32 [256, 128, 512], P('tile', 'gz')
The draws below stay inside these ranges and needn't reach their ends.
Inputs may be any that keep to these rules, and one draw needn't show every extreme that they name: `well_cell`: each value indexes a cell as (x * 16 + z) * 512 + y inside the block of 16 x 16 x 512 cells of its row's tile index and its column's gz index; several wells may share a cell.
All inputs are finite; a program needn't handle non-finite values.
Results may differ from the reference program's by a relative error of at most 0.0003.
Values sent between devices are 32-bit elements; how exact they have to be, the bound alone decides.
A program may use at most 192 MiB of HBM per device.

```python
import math
import jax
import jax.numpy as jnp
from jax import lax

CX = 16
CZ = 16
NY = 512
WELLS = 16
SWEEPS = 4
COARSE_ITERS = 6
NX = 256
NZ = 128
WELL_ROWS = 256
N_GZ = 8


def rough_field(key, low, high):
    logs = jax.random.uniform(key, (NX, NZ, NY), jnp.float32, math.log(low), math.log(high))
    return jnp.exp(logs)


def draw_trans_x(key, part):
    key = jax.random.fold_in(key, 11)
    return rough_field(key, 3.0, 10.0)


def draw_trans_y(key, part):
    key = jax.random.fold_in(key, 23)
    return rough_field(key, 0.5, 2.0)


def draw_trans_z(key, part):
    key = jax.random.fold_in(key, 37)
    return rough_field(key, 0.1, 0.3)


def draw_source(key, part):
    key = jax.random.fold_in(key, 41)
    return jax.random.truncated_normal(key, -6.0, 6.0, (NX, NZ, NY), jnp.float32)


def touch_ends(drawn, own_key, low, high):
    shape = drawn.shape
    place = [jax.random.randint(jax.random.fold_in(own_key, axis), (), 0, shape[axis]) for axis in range(len(shape))]
    drawn = drawn.at[tuple(place)].set(low)
    longest = shape.index(max(shape))
    place[longest] = (place[longest] + 1) % shape[longest]
    return drawn.at[tuple(place)].set(high)


def shard_levels(own_key, shape, cuts, smallest, high):
    loudness = 1.0
    for axis_at, shards_of in cuts:
        draws = jax.random.uniform(jax.random.fold_in(jax.random.fold_in(own_key, 6), axis_at), (shards_of,), jnp.float32, smallest / len(cuts), high / len(cuts))
        loudness = loudness * jnp.repeat(jnp.exp(draws), shape[axis_at] // shards_of).reshape((-1,) + (1,) * (len(shape) - 1 - axis_at))
    return loudness


def centred(stream_key, shape, scale, bound, cuts=(), kind=jnp.bfloat16):
    values = jax.random.normal(stream_key, shape, jnp.float32) * scale
    if len(cuts) > 0:
        values = shard_levels(stream_key, shape, cuts, -0.22, 0.18) * values
    return jnp.clip(values, min=-bound, max=bound).astype(kind)


def setup_inputs(seed: int = 0) -> dict:
    splits = jax.random.split(jax.random.key(seed), 8)
    return {
        "trans_x": draw_trans_x(jax.random.fold_in(splits[7], 71), 0),
        "trans_y": draw_trans_y(jax.random.fold_in(splits[7], 71), 0),
        "trans_z": draw_trans_z(jax.random.fold_in(splits[7], 71), 0),
        "accumulation": jnp.clip(jnp.exp(math.log(0.2) - 2.3025851 * jax.random.uniform(splits[3], (NX, NZ, NY), jnp.float32) ** shard_levels(splits[3], (NX, NZ, NY), ((0, 16), (1, 8)), -0.2, 0.2)), 0.02, 0.2),
        "source": draw_source(jax.random.fold_in(splits[7], 71), 0),
        "well_cell": touch_ends(jax.random.randint(splits[5], (WELL_ROWS, N_GZ), 0, CX * CZ * NY), jax.random.fold_in(splits[5], 1), 0, (CX * CZ * NY) - 1).astype(jnp.int32),
        "well_rate": centred(splits[6], (WELL_ROWS, N_GZ), 8.0, 48.0, ((0, 16), (1, 8)), jnp.float32),
    }


OMEGA = 2.0 / 3.0
COARSE_STEP = 0.5


def axis_nodes(position, extent):
    block = position // 8
    upper = (position % 8) >= 4
    rows = [block + jnp.where(block % 2 == parity, 0, jnp.where(upper, 1, -1)) for parity in (0, 1)]
    nodes = jnp.stack(rows).astype(jnp.int32)
    inside = (nodes >= 0) & (nodes < extent // 8)
    return nodes, inside


def axis_geometry(position, extent):
    nodes, inside = axis_nodes(position, extent)
    after, unused_after = axis_nodes(position + 1, extent)
    before, unused_before = axis_nodes(position - 1, extent)
    has_after = position + 1 < extent
    has_before = position >= 1
    same_after = (after == nodes).astype(jnp.float32)
    same_before = (before == nodes).astype(jnp.float32)
    inner = ((after == nodes) | ~has_after[None]) & ((before == nodes) | ~has_before[None])
    offsets = nodes - (position // 8)[None]
    edge_after = (((position + 1) % 8 == 0) & has_after).astype(jnp.float32)
    edge_before = (((position % 8) == 0) & has_before).astype(jnp.float32)
    return (inside.astype(jnp.float32), inner.astype(jnp.float32), same_after, same_before,
            offsets, edge_after, edge_before, has_after.astype(jnp.float32))


def spread_slots(pair, axis):
    picks = []
    for slot in range(8):
        digit = (slot // 4) if axis == 1 else ((slot // 2) % 2 if axis == 2 else slot % 2)
        picks.append(pair[digit])
    shape = [8, 1, 1, 1]
    shape[axis] = pair.shape[1]
    return jnp.stack(picks).reshape(shape)


def along(vector, axis):
    shape = [1, 1, 1]
    shape[axis] = vector.shape[0]
    return vector.reshape(shape)


def flux_apply(padded, faces, sames):
    center = padded[..., 1:-1, 1:-1, :]
    zero_col = jnp.zeros_like(center[..., :1])
    neighbours = (padded[..., 2:, 1:-1, :], padded[..., :-2, 1:-1, :],
                  padded[..., 1:-1, 2:, :], padded[..., 1:-1, :-2, :],
                  jnp.concatenate([center[..., 1:], zero_col], -1),
                  jnp.concatenate([zero_col, center[..., :-1]], -1))
    result = faces[0] * (center - sames[0] * neighbours[0])
    for index in range(1, 6):
        result = result + faces[index] * (center - sames[index] * neighbours[index])
    return result


def block_sum(field):
    size_x, size_z, size_y = field.shape
    return field.reshape(size_x // 8, 8, size_z // 8, 8, size_y // 8, 8).sum(axis=(1, 3, 5))


def one_hot_offsets(offsets):
    table = (offsets[:, :, None] == jnp.arange(-1, 2, dtype=jnp.int32)[None, None]).astype(jnp.float32)
    return table.reshape(2, offsets.shape[1] // 8, 8, 3)


def coarse_operator(edge_term, off_x, off_z, off_y):
    size_x, size_z, size_y = edge_term.shape[1:]
    shaped = edge_term.reshape(2, 2, 2, size_x // 8, 8, size_z // 8, 8, size_y // 8, 8)
    return jnp.einsum('abcIiKkJj,aIix,bKkz,cJjy->xzyIKJ', shaped, one_hot_offsets(off_x),
                      one_hot_offsets(off_z), one_hot_offsets(off_y), precision=lax.Precision.HIGHEST)


def apply_coarse(coarse_op, padded):
    full = jnp.pad(padded, ((0, 0), (0, 0), (1, 1)))
    count_x = padded.shape[0] - 2
    count_z = padded.shape[1] - 2
    count_y = padded.shape[2]
    result = jnp.zeros((count_x, count_z, count_y), jnp.float32)
    for ix in range(3):
        for iz in range(3):
            for iy in range(3):
                result = result + coarse_op[ix, iz, iy] * full[ix:ix + count_x, iz:iz + count_z, iy:iy + count_y]
    return result


def selection(offsets, padded_count):
    local = jnp.arange(offsets.shape[1], dtype=jnp.int32) // 8
    target = local[None] + 1 + offsets
    return (target[:, :, None] == jnp.arange(padded_count, dtype=jnp.int32)[None, None]).astype(jnp.float32)


def prolong(basis, padded_coarse, off_x, off_z, off_y):
    size_x, size_z, size_y = basis.shape[1:]
    values = jnp.einsum('aXi,bZk,cYj,ikj->abcXZY', selection(off_x, padded_coarse.shape[0]),
                        selection(off_z, padded_coarse.shape[1]), selection(off_y, padded_coarse.shape[2] + 2),
                        jnp.pad(padded_coarse, ((0, 0), (0, 0), (1, 1))), precision=lax.Precision.HIGHEST)
    return jnp.sum(basis * values.reshape(8, size_x, size_z, size_y), axis=0)


def reference(trans_x, trans_y, trans_z, accumulation, source, well_cell, well_rate):
    geo_x = axis_geometry(jnp.arange(NX, dtype=jnp.int32), NX)
    geo_z = axis_geometry(jnp.arange(NZ, dtype=jnp.int32), NZ)
    geo_y = axis_geometry(jnp.arange(NY, dtype=jnp.int32), NY)
    tx = trans_x * along(geo_x[7], 0)
    tz = trans_z * along(geo_z[7], 1)
    ty = trans_y * along(geo_y[7], 2)
    tx_prev = jnp.concatenate([jnp.zeros_like(tx[:1]), tx[:-1]], 0)
    tz_prev = jnp.concatenate([jnp.zeros_like(tz[:, :1]), tz[:, :-1]], 1)
    ty_prev = jnp.concatenate([jnp.zeros_like(ty[:, :, :1]), ty[:, :, :-1]], 2)
    faces = (tx, tx_prev, tz, tz_prev, ty, ty_prev)
    diagonal = tx + tx_prev + tz + tz_prev + ty + ty_prev
    valid = spread_slots(geo_x[0], 1) * spread_slots(geo_z[0], 2) * spread_slots(geo_y[0], 3)
    inner = valid * spread_slots(geo_x[1], 1) * spread_slots(geo_z[1], 2) * spread_slots(geo_y[1], 3)
    sames = (spread_slots(geo_x[2], 1), spread_slots(geo_x[3], 1), spread_slots(geo_z[2], 2),
             spread_slots(geo_z[3], 2), spread_slots(geo_y[2], 3), spread_slots(geo_y[3], 3))
    ones = (1.0, 1.0, 1.0, 1.0, 1.0, 1.0)
    basis = valid * spread_slots((geo_x[4] == 0).astype(jnp.float32), 1) * spread_slots(
        (geo_z[4] == 0).astype(jnp.float32), 2) * spread_slots((geo_y[4] == 0).astype(jnp.float32), 3)
    for sweep in range(SWEEPS):
        padded = jnp.pad(basis, ((0, 0), (1, 1), (1, 1), (0, 0)))
        flow = flux_apply(padded, faces, sames)
        basis = basis - OMEGA * inner * flow / diagonal
        basis = basis / jnp.sum(basis, axis=0)
    padded = jnp.pad(basis, ((0, 0), (1, 1), (1, 1), (0, 0)))
    block_faces = (tx * along(geo_x[5], 0), tx_prev * along(geo_x[6], 0), tz * along(geo_z[5], 1),
                   tz_prev * along(geo_z[6], 1), ty * along(geo_y[5], 2), ty_prev * along(geo_y[6], 2))
    edge_term = accumulation * basis + flux_apply(padded, block_faces, ones)
    coarse_op = coarse_operator(edge_term, geo_x[4], geo_z[4], geo_y[4])
    rows = (jnp.arange(well_cell.shape[0], dtype=jnp.int32) // WELLS)[:, None]
    columns = jnp.arange(well_cell.shape[1], dtype=jnp.int32)[None, :]
    cell_x = rows * CX + well_cell // (CZ * NY)
    cell_z = columns * CZ + (well_cell // NY) % CZ
    cell_y = well_cell % NY
    flat = ((cell_x * NZ + cell_z) * NY + cell_y).astype(jnp.int32).reshape(-1)
    rhs = source.reshape(-1).at[flat].add(well_rate.reshape(-1)).reshape(NX, NZ, NY)
    coarse_rhs = block_sum(rhs)
    coarse_scale = block_sum(accumulation + block_faces[0] + block_faces[1] + block_faces[2]
                             + block_faces[3] + block_faces[4] + block_faces[5])
    coarse = jnp.zeros_like(coarse_rhs)
    for step in range(COARSE_ITERS):
        coarse_pad = jnp.pad(coarse, ((1, 1), (1, 1), (0, 0)))
        coarse = coarse + COARSE_STEP * (coarse_rhs - apply_coarse(coarse_op, coarse_pad)) / coarse_scale
    coarse_pad = jnp.pad(coarse, ((1, 1), (1, 1), (0, 0)))
    pressure = prolong(basis, coarse_pad, geo_x[4], geo_z[4], geo_y[4])
    pressure_pad = jnp.pad(pressure, ((1, 1), (1, 1), (0, 0)))
    residual = rhs - (accumulation * pressure + flux_apply(pressure_pad, faces, ones))
    return basis, pressure, residual
```

```python
import jax
import jax.numpy as jnp
from jax import lax
from jax.experimental import pallas as pl
from jax.experimental.pallas import tpu as pltpu
from jax.sharding import PartitionSpec as P

COARSE_ITERS = 6
COARSE_STEP = 0.5
NT = 4
NXE = 24
NR = 32
F32 = jnp.float32
INTERPRET = False


def iota(shape, dim):
    return lax.broadcasted_iota(jnp.int32, shape, dim)


def roll(value, shift):
    return pltpu.roll(value, shift, 1)


def main_kernel(txe, tye, tze, acc, src, wcell, wrate,
                basis_out, coarse_out, rhs_out, xh_out, zh_out,
                tx_s, ty_s, tz_s, tym_s, dd_s, b0, b1, sums, sem_in, sem_out, sem_x):
    loads = []
    for t in range(NT):
        lanes = pl.ds(128 * t, 128)
        for k, (hbm, vmem) in enumerate(((txe, tx_s), (tye, ty_s), (tze, tz_s))):
            copy = pltpu.make_async_copy(hbm.at[:, :, lanes], vmem.at[:, t], sem_in.at[k * NT + t])
            copy.start()
            loads.append(copy)
    rhs_out[...] = src[...]
    lane_y = iota((1, 512), 1)
    for w in range(16):
        cell = wcell[w, 0]
        row = cell // 512
        x, z, y = row // 16, row % 16, cell % 512
        old = rhs_out[x, pl.ds(z, 1), :]
        rhs_out[x, pl.ds(z, 1), :] = old + jnp.where(lane_y == y, wrate[w, 0], 0.0)
    for copy in loads:
        copy.wait()

    sub = iota((8, 128), 0)
    lane = iota((8, 128), 1)
    yo = lane % 8
    lane_par = (lane // 8) % 2
    zero = jnp.zeros((8, 128), F32)

    def to_prev(value, left):
        return roll(jnp.where(lane == 127, left, value), 1)

    def to_next(value, right):
        return roll(jnp.where(lane == 0, right, value), 127)

    def first(index, carry):
        X, t = index // NT, index % NT
        tl = jnp.maximum(t - 1, 0)
        par = ((X + 4) // 8 + 1) % 2
        xo = (X + 4) % 8
        own_base, flip_base = par * 4, 4 - par * 4
        lo_x = (xo == 0).astype(F32)
        hi_x = (xo == 7).astype(F32)
        for r in range(3):
            R = 4 + 8 * r
            rows = pl.ds(R, 8)
            tx, txm = tx_s[X + 1, t, rows, :], tx_s[X, t, rows, :]
            tz, tzm = tz_s[X, t, rows, :], tz_s[X, t, pl.ds(R - 1, 8), :]
            ty = ty_s[X, t, rows, :]
            tym = to_prev(ty, ty_s[X, tl, rows, :])
            tym = jnp.where((lane == 0) & (t == 0), 0.0, tym)
            diag = tx + txm + tz + tzm + ty + tym
            half = diag * 0.5 + 1e-30
            tym_s[X, t, rows, :] = tym
            dd_s[X, t, rows, :] = half
            txb = lo_x * txm + hi_x * tx
            tzb = jnp.where(sub == 3, tz, jnp.where(sub == 4, tzm, 0.0))
            tyb = jnp.where(yo == 7, ty, jnp.where(yo == 0, tym, 0.0))
            own = half + (diag - txb - tzb - tyb)
            inv = 1.0 / (own + txb + tzb + tyb)
            own, vx, vz, vy = own * inv, txb * inv, tzb * inv, tyb * inv
            row_par = jnp.where(sub < 4, (r + 1) % 2, r % 2)
            for c in range(2):
                for d in range(2):
                    in_row, in_lane = row_par == c, lane_par == d
                    value = jnp.where(in_row, jnp.where(in_lane, own, vy), jnp.where(in_lane, vz, 0.0))
                    b0[own_base + 2 * c + d, X, t, rows, :] = value
                    b0[flip_base + 2 * c + d, X, t, rows, :] = jnp.where(in_row & in_lane, vx, 0.0)
                    b1[flip_base + 2 * c + d, X, t, rows, :] = zero
        return carry

    lax.fori_loop(0, NXE * NT, first, 0)

    def sweep(old, new, k):
        reach = min(k, 3)

        def block(X, t, n_slots, par):
            tl, tr = jnp.maximum(t - 1, 0), jnp.minimum(t + 1, NT - 1)
            own_base, flip_base = par * 4, 4 - par * 4
            for r in range(3):
                R = 4 + 8 * r
                rows = pl.ds(R, 8)
                tx, txm = tx_s[X + 1, t, rows, :], tx_s[X, t, rows, :]
                tz, tzm = tz_s[X, t, rows, :], tz_s[X, t, pl.ds(R - 1, 8), :]
                ty, tym = ty_s[X, t, rows, :], tym_s[X, t, rows, :]
                half = dd_s[X, t, rows, :]
                row_par = jnp.where(sub < 4, (r + 1) % 2, r % 2)
                values = []
                for cd in range(n_slots):
                    c, d = (cd // 2) % 2, cd % 2
                    s = (own_base if cd < 4 else flip_base) + cd % 4
                    b = old[s, X, t, rows, :]
                    v = half * b
                    v += tx * old[s, X + 1, t, rows, :]
                    v += txm * old[s, X - 1, t, rows, :]
                    v += tz * old[s, X, t, pl.ds(R + 1, 8), :]
                    v += tzm * old[s, X, t, pl.ds(R - 1, 8), :]
                    v += ty * to_next(b, old[s, X, tr, rows, :])
                    v += tym * to_prev(b, old[s, X, tl, rows, :])
                    if k == 4:
                        out_z = (row_par != c) & ((sub == 0) | (sub == 7))
                        out_y = (lane_par != d) & ((yo == 3) | (yo == 4))
                        v = jnp.where(out_z | out_y, 0.0, v)
                    values.append(v)
                total = values[0]
                for v in values[1:]:
                    total = total + v
                inv = 1.0 / total
                for cd in range(n_slots):
                    s = (own_base if cd < 4 else flip_base) + cd % 4
                    new[s, X, t, rows, :] = values[cd] * inv

        def step(index, carry):
            X, t = index // NT, index % NT
            par = ((X + 4) // 8 + 1) % 2
            xo = (X + 4) % 8
            dist = jnp.where(xo < 4, xo + 1, 8 - xo)

            @pl.when(dist <= reach)
            def _():
                block(X, t, 8, par)

            @pl.when(dist > reach)
            def _():
                block(X, t, 4, par)

            return carry

        lax.fori_loop((k - 1) * NT, (25 - k) * NT, step, 0)

    sweep(b0, b1, 2)
    sweep(b1, b0, 3)
    sweep(b0, b1, 4)

    stores = []
    for s in range(8):
        for t in range(NT):
            copy = pltpu.make_async_copy(b1.at[s, pl.ds(4, 16), t, pl.ds(8, 16), :],
                                         basis_out.at[s, :, :, pl.ds(128 * t, 128)], sem_out.at[s * NT + t])
            copy.start()
            stores.append(copy)
            for side, X in enumerate((3, 20)):
                copy = pltpu.make_async_copy(b1.at[s, X, t, pl.ds(8, 16), :],
                                             xh_out.at[s, side, :, pl.ds(128 * t, 128)],
                                             sem_x.at[(s * NT + t) * 2 + side])
                copy.start()
                stores.append(copy)

    flat = b1.reshape(8 * NXE * NT * NR, 128)

    def rows_of(index, carry):
        s, t = index // NT, index % NT
        lanes = pl.ds(pl.multiple_of(t * 128, 128), 128)
        for side, R in enumerate((7, 24)):
            for half in range(2):
                start = ((s * NXE + 4 + 8 * half) * NT + t) * NR + R
                zh_out[s, side, 8 * half:8 * half + 8, lanes] = flat[pl.ds(start, 8, stride=NT * NR), :]
        return carry

    lax.fori_loop(0, 8 * NT, rows_of, 0)

    for zb in range(2):
        R = 8 + 8 * zb

        def edges(index, carry):
            xb, t = index // NT, index % NT
            tl, tr = jnp.maximum(t - 1, 0), jnp.minimum(t + 1, NT - 1)
            rows = pl.ds(R, 8)
            lanes = pl.ds(pl.multiple_of(t * 128, 128), 128)
            own_base, flip_base = xb * 4, 4 - xb * 4
            groups = [[None] * 4 for _ in range(3)]
            scale = zero
            right = zero
            for xo in range(8):
                X = 4 + xb * 8 + xo
                x = xb * 8 + xo
                tz, tzm = tz_s[X, t, rows, :], tz_s[X, t, pl.ds(R - 1, 8), :]
                ty, tym = ty_s[X, t, rows, :], tym_s[X, t, rows, :]
                tzb = jnp.where(sub == 7, tz, jnp.where(sub == 0, tzm, 0.0))
                tyb = jnp.where(yo == 7, ty, jnp.where(yo == 0, tym, 0.0))
                central = acc[x, 8 * zb:8 * zb + 8, lanes] + tzb + tyb
                if xo == 0:
                    txb, xn = tx_s[X, t, rows, :], X - 1
                    central = central + txb
                if xo == 7:
                    txb, xn = tx_s[X + 1, t, rows, :], X + 1
                    central = central + txb
                scale = scale + central
                right = right + rhs_out[x, 8 * zb:8 * zb + 8, lanes]
                which = [(0, own_base)]
                if xo < 3:
                    which.append((1, flip_base))
                if xo > 4:
                    which.append((2, flip_base))
                for g, base in which:
                    for cd in range(4):
                        s = base + cd
                        b = b1[s, X, t, rows, :]
                        bz = jnp.where(sub == 7, b1[s, X, t, pl.ds(R + 1, 8), :], b1[s, X, t, pl.ds(R - 1, 8), :])
                        by = jnp.where(yo == 7, to_next(b, b1[s, X, tr, rows, :]), to_prev(b, b1[s, X, tl, rows, :]))
                        e = central * b - tzb * bz - tyb * by
                        if xo in (0, 7):
                            e = e - txb * b1[s, xn, t, rows, :]
                        groups[g][cd] = e if groups[g][cd] is None else groups[g][cd] + e
            for g in range(3):
                for cd in range(4):
                    u = xb * 12 + g * 4 + cd
                    sums[t, pl.ds(pl.multiple_of(u * 16 + 8 * zb, 8), 8), :] = groups[g][cd]
            sums[t, pl.ds(pl.multiple_of((24 + xb) * 16 + 8 * zb, 8), 8), :] = scale
            sums[t, pl.ds(pl.multiple_of((26 + xb) * 16 + 8 * zb, 8), 8), :] = right
            return carry

        lax.fori_loop(0, 2 * NT, edges, 0)

    l_y, l_j = iota((128, 128), 0), iota((128, 128), 1)
    folded = jnp.zeros((448, 128), F32)
    for t in range(NT):
        target = ((l_y % 8) // 4) * 64 + 16 * t + l_y // 8
        folded = folded + jnp.dot(sums[t], (l_j == target).astype(F32), precision=lax.Precision.HIGHEST,
                                  preferred_element_type=F32)
    o, i = iota((128, 448), 0), iota((128, 448), 1)
    pick = ((i // 16 == o % 32) & ((i % 16) // 4 == o // 32)).astype(F32)
    quarters = jnp.dot(pick, folded, precision=lax.Precision.HIGHEST, preferred_element_type=F32)

    lane1 = iota((1, 128), 1)
    odd = lane1 % 2 == 1
    low = lane1 < 64

    def unit(q, u):
        return quarters[q * 32 + u:q * 32 + u + 1, :]

    def halves(value):
        return value + roll(value, 64)

    for xb in range(2):
        for dx, g in ((0, 1), (1, 0), (2, 2)):
            for dz in range(3):
                parts = []
                for zb in range(2):
                    c = zb if dz == 1 else 1 - zb
                    vs = []
                    for d in range(2):
                        u = xb * 12 + g * 4 + c * 2 + d
                        if dz == 0:
                            vs.append(unit(2 * zb, u))
                        elif dz == 2:
                            vs.append(unit(2 * zb + 1, u))
                        else:
                            vs.append(unit(2 * zb, u) + unit(2 * zb + 1, u))
                    own = jnp.where(odd, vs[1], vs[0])
                    flip = jnp.where(odd, vs[0], vs[1])
                    turned = roll(flip, 64)
                    parts.append((flip, halves(own), turned) if zb == 0 else (turned, halves(own), flip))
                for dy in range(3):
                    k = dx * 9 + dz * 3 + dy
                    coarse_out[xb, k:k + 1, :] = jnp.where(low, parts[0][dy], parts[1][dy])
        for k, u in ((27, 26 + xb), (28, 24 + xb)):
            parts = [halves(unit(2 * zb, u) + unit(2 * zb + 1, u)) for zb in range(2)]
            coarse_out[xb, k:k + 1, :] = jnp.where(low, parts[0], parts[1])
        coarse_out[xb, 29:32, :] = jnp.zeros((3, 128), F32)

    for copy in stores:
        copy.wait()


def finish_kernel(txe, tye, tze, basis, xh, zh, c4, acc, rhs, pressure_out, residual_out,
                  tx_s, ty_s, tz_s, g_s, p_s, sem_in):
    loads = []
    for t in range(NT):
        lanes = pl.ds(128 * t, 128)
        for k, (hbm, vmem) in enumerate(((txe.at[pl.ds(4, 17)], tx_s), (tye.at[pl.ds(4, 16)], ty_s),
                                         (tze.at[pl.ds(4, 16)], tz_s))):
            copy = pltpu.make_async_copy(hbm.at[:, pl.ds(0, 24), lanes], vmem.at[:, t], sem_in.at[k * NT + t])
            copy.start()
            loads.append(copy)
    sub = iota((8, 128), 0)
    lane = iota((8, 128), 1)
    upper = sub >= 4

    j, y = iota((128, 512), 0), iota((128, 512), 1)
    block = y // 8
    side = jnp.where(y % 8 >= 4, 1, -1)
    spread = []
    for d in range(2):
        node = jnp.where(block % 2 == d, block, block + side)
        spread.append(jnp.dot(c4[...], (j == node).astype(F32), precision=lax.Precision.HIGHEST,
                              preferred_element_type=F32))
    for nx in range(4):
        for c in range(2):
            for d in range(2):
                def row(nz):
                    return spread[d][nx * 4 + nz:nx * 4 + nz + 1, :]
                if c == 0:
                    tiles = (row(1), row(1)), (row(1), row(3))
                else:
                    tiles = (row(0), row(2)), (row(2), row(2))
                for zb in range(2):
                    for t in range(NT):
                        a, b = (jnp.broadcast_to(v[:, 128 * t:128 * t + 128], (8, 128)) for v in tiles[zb])
                        g_s[nx, 2 * c + d, t, 8 * zb:8 * zb + 8, :] = jnp.where(upper, b, a)

    def plane_nodes(X):
        block_x = (X + 4) // 8 - 1
        par = (block_x + 2) % 2
        up = (X + 4) % 8 >= 4
        flip = block_x + 1 + jnp.where(up, 1, -1)
        own = block_x + 1
        return jnp.where(par == 0, own, flip), jnp.where(par == 0, flip, own)

    def prolong(read, X, t, zb):
        n0, n1 = plane_nodes(X)
        total = None
        for s in range(8):
            n = n0 if s < 4 else n1
            term = read(s) * g_s[n, s % 4, t, 8 * zb:8 * zb + 8, :]
            total = term if total is None else total + term
        return total

    def pressures(index, carry):
        x, t = index // NT, index % NT
        lanes = pl.ds(pl.multiple_of(t * 128, 128), 128)
        for zb in range(2):
            p = prolong(lambda s: basis[s, x, 8 * zb:8 * zb + 8, lanes], x + 4, t, zb)
            p_s[x + 1, t, 8 + 8 * zb:16 + 8 * zb, :] = p
            pressure_out[x, 8 * zb:8 * zb + 8, lanes] = p
        return carry

    lax.fori_loop(0, 16 * NT, pressures, 0)

    def outer(t, carry):
        lanes = pl.ds(pl.multiple_of(t * 128, 128), 128)
        for zb in range(2):
            for s_x, X, at in ((0, 3, 0), (1, 20, 17)):
                p = prolong(lambda s: xh[s, s_x, 8 * zb:8 * zb + 8, lanes], X, t, zb)
                p_s[at, t, 8 + 8 * zb:16 + 8 * zb, :] = p
        return carry

    lax.fori_loop(0, NT, outer, 0)
    flat = p_s.reshape(18 * NT * NR, 128)
    for t in range(NT):
        cols = slice(128 * t, 128 * t + 128)
        for s_z, R in ((0, 7), (1, 24)):
            for half in range(2):
                total = None
                for s in range(8):
                    a, c, d = s // 4, (s // 2) % 2, s % 2
                    nz = (1, 0)[c] if s_z == 0 else (3, 2)[c]
                    def row(nx):
                        return jnp.broadcast_to(spread[d][nx * 4 + nz:nx * 4 + nz + 1, cols], (8, 128))
                    if a == 0:
                        value = row(1) if half == 0 else jnp.where(upper, row(3), row(1))
                    else:
                        value = jnp.where(upper, row(2), row(0)) if half == 0 else row(2)
                    term = zh[s, s_z, 8 * half:8 * half + 8, cols] * value
                    total = term if total is None else total + term
                flat[pl.ds(((1 + 8 * half) * NT + t) * NR + R, 8, stride=NT * NR), :] = total
    for copy in loads:
        copy.wait()

    def to_prev(value, left):
        return roll(jnp.where(lane == 127, left, value), 1)

    def to_next(value, right):
        return roll(jnp.where(lane == 0, right, value), 127)

    def residuals(index, carry):
        x, t = index // NT, index % NT
        lanes = pl.ds(pl.multiple_of(t * 128, 128), 128)
        tl, tr = jnp.maximum(t - 1, 0), jnp.minimum(t + 1, NT - 1)
        for zb in range(2):
            R = 8 + 8 * zb
            rows = pl.ds(R, 8)
            p = p_s[x + 1, t, rows, :]
            ty = ty_s[x, t, rows, :]
            tym = jnp.where((lane == 0) & (t == 0), 0.0, to_prev(ty, ty_s[x, tl, rows, :]))
            flow = acc[x, 8 * zb:8 * zb + 8, lanes] * p
            flow += tx_s[x + 1, t, rows, :] * (p - p_s[x + 2, t, rows, :])
            flow += tx_s[x, t, rows, :] * (p - p_s[x, t, rows, :])
            flow += tz_s[x, t, rows, :] * (p - p_s[x + 1, t, pl.ds(R + 1, 8), :])
            flow += tz_s[x, t, pl.ds(R - 1, 8), :] * (p - p_s[x + 1, t, pl.ds(R - 1, 8), :])
            flow += ty * (p - to_next(p, p_s[x + 1, tr, rows, :]))
            flow += tym * (p - to_prev(p, p_s[x + 1, tl, rows, :]))
            residual_out[x, 8 * zb:8 * zb + 8, lanes] = rhs[x, 8 * zb:8 * zb + 8, lanes] - flow
        return carry

    lax.fori_loop(0, 16 * NT, residuals, 0)


VMEM_SPEC = pl.BlockSpec(memory_space=pltpu.VMEM)
SMEM_SPEC = pl.BlockSpec(memory_space=pltpu.SMEM)
ANY_SPEC = pl.BlockSpec(memory_space=pl.ANY)


def run_main(txe, tye, tze, acc, src, wcell, wrate):
    field = pltpu.VMEM((NXE, NT, NR, 128), F32)
    return pl.pallas_call(
        main_kernel,
        name="sweeps",
        out_shape=(jax.ShapeDtypeStruct((8, 16, 16, 512), F32), jax.ShapeDtypeStruct((2, 32, 128), F32),
                   jax.ShapeDtypeStruct((16, 16, 512), F32), jax.ShapeDtypeStruct((8, 2, 16, 512), F32),
                   jax.ShapeDtypeStruct((8, 2, 16, 512), F32)),
        in_specs=[ANY_SPEC] * 3 + [VMEM_SPEC] * 2 + [SMEM_SPEC] * 2,
        out_specs=(ANY_SPEC, VMEM_SPEC, VMEM_SPEC, ANY_SPEC, VMEM_SPEC),
        scratch_shapes=[
            pltpu.VMEM((NXE + 1, NT, NR, 128), F32), field, field, field, field,
            pltpu.VMEM((8, NXE, NT, NR, 128), F32), pltpu.VMEM((8, NXE, NT, NR, 128), F32),
            pltpu.VMEM((NT, 448, 128), F32),
            pltpu.SemaphoreType.DMA((3 * NT,)), pltpu.SemaphoreType.DMA((8 * NT,)),
            pltpu.SemaphoreType.DMA((16 * NT,)),
        ],
        compiler_params=pltpu.CompilerParams(vmem_limit_bytes=60 * 1024 * 1024),
        interpret=INTERPRET,
    )(txe, tye, tze, acc, src, wcell, wrate)


def run_finish(txe, tye, tze, basis, xh, zh, c4, acc, rhs):
    return pl.pallas_call(
        finish_kernel,
        name="finish",
        out_shape=(jax.ShapeDtypeStruct((16, 16, 512), F32), jax.ShapeDtypeStruct((16, 16, 512), F32)),
        in_specs=[ANY_SPEC] * 3 + [VMEM_SPEC] * 6,
        out_specs=(VMEM_SPEC, VMEM_SPEC),
        scratch_shapes=[
            pltpu.VMEM((17, NT, 24, 128), F32), pltpu.VMEM((16, NT, 24, 128), F32), pltpu.VMEM((16, NT, 24, 128), F32),
            pltpu.VMEM((4, 4, NT, 16, 128), F32), pltpu.VMEM((18, NT, NR, 128), F32),
            pltpu.SemaphoreType.DMA((3 * NT,)),
        ],
        compiler_params=pltpu.CompilerParams(vmem_limit_bytes=60 * 1024 * 1024),
        interpret=INTERPRET,
    )(txe, tye, tze, basis, xh, zh, c4, acc, rhs)


def shift_up(value, axis):
    size = lax.axis_size(axis)
    return lax.ppermute(value, axis, [(i, i + 1) for i in range(size - 1)])


def shift_down(value, axis):
    size = lax.axis_size(axis)
    return lax.ppermute(value, axis, [(i + 1, i) for i in range(size - 1)])


def extend(tx, ty, tz):
    up = jnp.concatenate([tx[:, 12:], ty[:, 12:], tz[:, 11:]], 1)
    down = jnp.concatenate([tx[:, :4], ty[:, :4], tz[:, :4]], 1)
    low, high = shift_up(up, "gz"), shift_down(down, "gz")
    fill = jnp.zeros((16, 4, 512), F32)
    txz = jnp.concatenate([low[:, :4], tx, high[:, :4]], 1)
    tyz = jnp.concatenate([low[:, 4:8], ty, high[:, 4:8]], 1)
    tzz = jnp.concatenate([low[:, 9:13], tz, high[:, 8:12]], 1)
    up = jnp.concatenate([txz[11:], tyz[12:], tzz[12:]], 0)
    down = jnp.concatenate([txz[:4], tyz[:4], tzz[:4]], 0)
    lowx, highx = shift_up(up, "tile"), shift_down(down, "tile")
    txe = jnp.pad(jnp.concatenate([lowx[:5], txz, highx[:4]], 0), ((0, 0), (4, 4), (0, 0)))
    tye = jnp.pad(jnp.concatenate([lowx[5:9], tyz, highx[4:8]], 0), ((0, 0), (4, 4), (0, 0)))
    tze = jnp.pad(jnp.concatenate([lowx[9:13], tzz, highx[8:12]], 0), ((0, 0), (4, 4), (0, 0)))
    extra = jnp.pad(low[:, 8:9], ((4, 4), (3, 28), (0, 0)))
    return txe, tye, tze + extra


def coarse_outer(value):
    for axis, dim in (("tile", 0), ("gz", 1)):
        head = lax.slice_in_dim(value, 0, 1, axis=dim)
        tail = lax.slice_in_dim(value, value.shape[dim] - 1, value.shape[dim], axis=dim)
        value = jnp.concatenate([shift_up(tail, axis), value, shift_down(head, axis)], axis=dim)
    return value


def coarse_solve(packed):
    op = packed[:, :27].reshape(2, 27, 2, 64).transpose(1, 0, 2, 3)
    right = packed[:, 27].reshape(2, 2, 64)
    scale = packed[:, 28].reshape(2, 2, 64)
    coarse = COARSE_STEP * right / scale
    for _ in range(COARSE_ITERS - 1):
        full = jnp.pad(coarse_outer(coarse), ((0, 0), (0, 0), (1, 1)))
        total = jnp.zeros((2, 2, 64), F32)
        for k in range(27):
            ix, iz, iy = k // 9, (k // 3) % 3, k % 3
            total = total + op[k] * full[ix:ix + 2, iz:iz + 2, iy:iy + 64]
        coarse = coarse + COARSE_STEP * (right - total) / scale
    return jnp.pad(coarse_outer(coarse).reshape(16, 64), ((0, 0), (0, 64)))


def body(trans_x, trans_y, trans_z, accumulation, source, well_cell, well_rate):
    last_x = lax.axis_index("tile") == lax.axis_size("tile") - 1
    last_z = lax.axis_index("gz") == lax.axis_size("gz") - 1
    tx = jnp.where((jnp.arange(16) == 15)[:, None, None] & last_x, 0.0, trans_x)
    tz = jnp.where((jnp.arange(16) == 15)[None, :, None] & last_z, 0.0, trans_z)
    ty = jnp.where((jnp.arange(512) == 511)[None, None, :], 0.0, trans_y)
    txe, tye, tze = extend(tx, ty, tz)
    basis, packed, rhs, xh, zh = run_main(txe, tye, tze, accumulation, source, well_cell, well_rate)
    c4 = coarse_solve(packed)
    pressure, residual = run_finish(txe, tye, tze, basis, xh, zh, c4, accumulation, rhs)
    return basis, pressure, residual


def solution(mesh):
    grid = P("tile", "gz", None)
    return jax.shard_map(
        body,
        mesh=mesh,
        in_specs=(grid,) * 5 + (P("tile", "gz"),) * 2,
        out_specs=(P(None, "tile", "gz", None), grid, grid),
        check_vma=False,
    )
```

```python
import jax
import jax.numpy as jnp
from jax import lax
from jax.experimental import pallas as pl
from jax.experimental.pallas import tpu as pltpu
from jax.sharding import PartitionSpec as P

COARSE_STEP = 0.5
NT = 4
NXE = 24
NR = 32
F32 = jnp.float32
INTERPRET = False
COMM_INTERPRET = False


def iota(shape, dim):
    return lax.broadcasted_iota(jnp.int32, shape, dim)


def roll(value, shift):
    return pltpu.roll(value, shift, 1)


def main_kernel(txe, tye, tze, acc, src, wcell, wrate,
                basis_out, coarse_out, rhs_out, xh_out, zh_out,
                tx_s, ty_s, tz_s, tym_s, dd_s, b0, b1, sums, sem_in, sem_out, sem_x):
    loads = []
    for t in range(NT):
        lanes = pl.ds(128 * t, 128)
        for k, (hbm, vmem) in enumerate(((txe, tx_s), (tye, ty_s), (tze, tz_s))):
            copy = pltpu.make_async_copy(hbm.at[:, :, lanes], vmem.at[:, t], sem_in.at[k * NT + t])
            copy.start()
            loads.append(copy)
    rhs_out[...] = src[...]
    lane_y = iota((1, 512), 1)
    for w in range(16):
        cell = wcell[w, 0]
        row = cell // 512
        x, z, y = row // 16, row % 16, cell % 512
        old = rhs_out[x, pl.ds(z, 1), :]
        rhs_out[x, pl.ds(z, 1), :] = old + jnp.where(lane_y == y, wrate[w, 0], 0.0)
    for copy in loads:
        copy.wait()

    sub = iota((8, 128), 0)
    lane = iota((8, 128), 1)
    yo = lane % 8
    lane_par = (lane // 8) % 2
    zero = jnp.zeros((8, 128), F32)

    def to_prev(value, left):
        return roll(jnp.where(lane == 127, left, value), 1)

    def to_next(value, right):
        return roll(jnp.where(lane == 0, right, value), 127)

    def first(index, carry):
        X, t = index // NT, index % NT
        tl = jnp.maximum(t - 1, 0)
        par = ((X + 4) // 8 + 1) % 2
        xo = (X + 4) % 8
        own_base, flip_base = par * 4, 4 - par * 4
        lo_x = (xo == 0).astype(F32)
        hi_x = (xo == 7).astype(F32)
        for r in range(3):
            R = 4 + 8 * r
            rows = pl.ds(R, 8)
            tx, txm = tx_s[X + 1, t, rows, :], tx_s[X, t, rows, :]
            tz, tzm = tz_s[X, t, rows, :], tz_s[X, t, pl.ds(R - 1, 8), :]
            ty = ty_s[X, t, rows, :]
            tym = to_prev(ty, ty_s[X, tl, rows, :])
            tym = jnp.where((lane == 0) & (t == 0), 0.0, tym)
            diag = tx + txm + tz + tzm + ty + tym
            half = diag * 0.5 + 1e-30
            tym_s[X, t, rows, :] = tym
            dd_s[X, t, rows, :] = half
            txb = lo_x * txm + hi_x * tx
            tzb = jnp.where(sub == 3, tz, jnp.where(sub == 4, tzm, 0.0))
            tyb = jnp.where(yo == 7, ty, jnp.where(yo == 0, tym, 0.0))
            own = half + (diag - txb - tzb - tyb)
            inv = 1.0 / (own + txb + tzb + tyb)
            own, vx, vz, vy = own * inv, txb * inv, tzb * inv, tyb * inv
            row_par = jnp.where(sub < 4, (r + 1) % 2, r % 2)
            for c in range(2):
                for d in range(2):
                    in_row, in_lane = row_par == c, lane_par == d
                    value = jnp.where(in_row, jnp.where(in_lane, own, vy), jnp.where(in_lane, vz, 0.0))
                    b0[own_base + 2 * c + d, X, t, rows, :] = value
                    b0[flip_base + 2 * c + d, X, t, rows, :] = jnp.where(in_row & in_lane, vx, 0.0)
                    b1[flip_base + 2 * c + d, X, t, rows, :] = zero
        return carry

    lax.fori_loop(0, NXE * NT, first, 0)

    def sweep(old, new, k):
        reach = min(k, 3)

        def block(X, t, n_slots, par):
            tl, tr = jnp.maximum(t - 1, 0), jnp.minimum(t + 1, NT - 1)
            own_base, flip_base = par * 4, 4 - par * 4
            for r in range(3):
                R = 4 + 8 * r
                rows = pl.ds(R, 8)
                tx, txm = tx_s[X + 1, t, rows, :], tx_s[X, t, rows, :]
                tz, tzm = tz_s[X, t, rows, :], tz_s[X, t, pl.ds(R - 1, 8), :]
                ty, tym = ty_s[X, t, rows, :], tym_s[X, t, rows, :]
                half = dd_s[X, t, rows, :]
                row_par = jnp.where(sub < 4, (r + 1) % 2, r % 2)
                values = []
                for cd in range(n_slots):
                    c, d = (cd // 2) % 2, cd % 2
                    s = (own_base if cd < 4 else flip_base) + cd % 4
                    b = old[s, X, t, rows, :]
                    v = half * b
                    v += tx * old[s, X + 1, t, rows, :]
                    v += txm * old[s, X - 1, t, rows, :]
                    v += tz * old[s, X, t, pl.ds(R + 1, 8), :]
                    v += tzm * old[s, X, t, pl.ds(R - 1, 8), :]
                    v += ty * to_next(b, old[s, X, tr, rows, :])
                    v += tym * to_prev(b, old[s, X, tl, rows, :])
                    if k == 4:
                        out_z = (row_par != c) & ((sub == 0) | (sub == 7))
                        out_y = (lane_par != d) & ((yo == 3) | (yo == 4))
                        v = jnp.where(out_z | out_y, 0.0, v)
                    values.append(v)
                total = values[0]
                for v in values[1:]:
                    total = total + v
                inv = 1.0 / total
                for cd in range(n_slots):
                    s = (own_base if cd < 4 else flip_base) + cd % 4
                    new[s, X, t, rows, :] = values[cd] * inv

        def step(index, carry):
            X, t = index // NT, index % NT
            par = ((X + 4) // 8 + 1) % 2
            xo = (X + 4) % 8
            dist = jnp.where(xo < 4, xo + 1, 8 - xo)

            @pl.when(dist <= reach)
            def _():
                block(X, t, 8, par)

            @pl.when(dist > reach)
            def _():
                block(X, t, 4, par)

            return carry

        lax.fori_loop((k - 1) * NT, (25 - k) * NT, step, 0)

    sweep(b0, b1, 2)
    sweep(b1, b0, 3)
    sweep(b0, b1, 4)

    stores = []
    for s in range(8):
        for t in range(NT):
            copy = pltpu.make_async_copy(b1.at[s, pl.ds(4, 16), t, pl.ds(8, 16), :],
                                         basis_out.at[s, :, :, pl.ds(128 * t, 128)], sem_out.at[s * NT + t])
            copy.start()
            stores.append(copy)
            for side, X in enumerate((3, 20)):
                copy = pltpu.make_async_copy(b1.at[s, X, t, pl.ds(8, 16), :],
                                             xh_out.at[s, side, :, pl.ds(128 * t, 128)],
                                             sem_x.at[(s * NT + t) * 2 + side])
                copy.start()
                stores.append(copy)

    flat = b1.reshape(8 * NXE * NT * NR, 128)

    def rows_of(index, carry):
        s, t = index // NT, index % NT
        lanes = pl.ds(pl.multiple_of(t * 128, 128), 128)
        for side, R in enumerate((7, 24)):
            for half in range(2):
                start = ((s * NXE + 4 + 8 * half) * NT + t) * NR + R
                zh_out[s, side, 8 * half:8 * half + 8, lanes] = flat[pl.ds(start, 8, stride=NT * NR), :]
        return carry

    lax.fori_loop(0, 8 * NT, rows_of, 0)

    for zb in range(2):
        R = 8 + 8 * zb

        def edges(index, carry):
            xb, t = index // NT, index % NT
            tl, tr = jnp.maximum(t - 1, 0), jnp.minimum(t + 1, NT - 1)
            rows = pl.ds(R, 8)
            lanes = pl.ds(pl.multiple_of(t * 128, 128), 128)
            own_base, flip_base = xb * 4, 4 - xb * 4
            groups = [[None] * 4 for _ in range(3)]
            scale = zero
            right = zero
            for xo in range(8):
                X = 4 + xb * 8 + xo
                x = xb * 8 + xo
                tz, tzm = tz_s[X, t, rows, :], tz_s[X, t, pl.ds(R - 1, 8), :]
                ty, tym = ty_s[X, t, rows, :], tym_s[X, t, rows, :]
                tzb = jnp.where(sub == 7, tz, jnp.where(sub == 0, tzm, 0.0))
                tyb = jnp.where(yo == 7, ty, jnp.where(yo == 0, tym, 0.0))
                central = acc[x, 8 * zb:8 * zb + 8, lanes] + tzb + tyb
                if xo == 0:
                    txb, xn = tx_s[X, t, rows, :], X - 1
                    central = central + txb
                if xo == 7:
                    txb, xn = tx_s[X + 1, t, rows, :], X + 1
                    central = central + txb
                scale = scale + central
                right = right + rhs_out[x, 8 * zb:8 * zb + 8, lanes]
                which = [(0, own_base)]
                if xo < 3:
                    which.append((1, flip_base))
                if xo > 4:
                    which.append((2, flip_base))
                for g, base in which:
                    for cd in range(4):
                        s = base + cd
                        b = b1[s, X, t, rows, :]
                        bz = jnp.where(sub == 7, b1[s, X, t, pl.ds(R + 1, 8), :], b1[s, X, t, pl.ds(R - 1, 8), :])
                        by = jnp.where(yo == 7, to_next(b, b1[s, X, tr, rows, :]), to_prev(b, b1[s, X, tl, rows, :]))
                        e = central * b - tzb * bz - tyb * by
                        if xo in (0, 7):
                            e = e - txb * b1[s, xn, t, rows, :]
                        groups[g][cd] = e if groups[g][cd] is None else groups[g][cd] + e
            for g in range(3):
                for cd in range(4):
                    u = xb * 12 + g * 4 + cd
                    sums[t, pl.ds(pl.multiple_of(u * 16 + 8 * zb, 8), 8), :] = groups[g][cd]
            sums[t, pl.ds(pl.multiple_of((24 + xb) * 16 + 8 * zb, 8), 8), :] = scale
            sums[t, pl.ds(pl.multiple_of((26 + xb) * 16 + 8 * zb, 8), 8), :] = right
            return carry

        lax.fori_loop(0, 2 * NT, edges, 0)

    l_y, l_j = iota((128, 128), 0), iota((128, 128), 1)
    folded = jnp.zeros((448, 128), F32)
    for t in range(NT):
        target = ((l_y % 8) // 4) * 64 + 16 * t + l_y // 8
        folded = folded + jnp.dot(sums[t], (l_j == target).astype(F32), precision=lax.Precision.HIGHEST,
                                  preferred_element_type=F32)
    o, i = iota((128, 448), 0), iota((128, 448), 1)
    pick = ((i // 16 == o % 32) & ((i % 16) // 4 == o // 32)).astype(F32)
    quarters = jnp.dot(pick, folded, precision=lax.Precision.HIGHEST, preferred_element_type=F32)

    lane1 = iota((1, 128), 1)
    odd = lane1 % 2 == 1
    low = lane1 < 64

    def unit(q, u):
        return quarters[q * 32 + u:q * 32 + u + 1, :]

    def halves(value):
        return value + roll(value, 64)

    for xb in range(2):
        for dx, g in ((0, 1), (1, 0), (2, 2)):
            for dz in range(3):
                parts = []
                for zb in range(2):
                    c = zb if dz == 1 else 1 - zb
                    vs = []
                    for d in range(2):
                        u = xb * 12 + g * 4 + c * 2 + d
                        if dz == 0:
                            vs.append(unit(2 * zb, u))
                        elif dz == 2:
                            vs.append(unit(2 * zb + 1, u))
                        else:
                            vs.append(unit(2 * zb, u) + unit(2 * zb + 1, u))
                    own = jnp.where(odd, vs[1], vs[0])
                    flip = jnp.where(odd, vs[0], vs[1])
                    turned = roll(flip, 64)
                    parts.append((flip, halves(own), turned) if zb == 0 else (turned, halves(own), flip))
                for dy in range(3):
                    k = dx * 9 + dz * 3 + dy
                    coarse_out[xb, k:k + 1, :] = jnp.where(low, parts[0][dy], parts[1][dy])
        for k, u in ((27, 26 + xb), (28, 24 + xb)):
            parts = [halves(unit(2 * zb, u) + unit(2 * zb + 1, u)) for zb in range(2)]
            coarse_out[xb, k:k + 1, :] = jnp.where(low, parts[0], parts[1])
        coarse_out[xb, 29:32, :] = jnp.zeros((3, 128), F32)

    for copy in stores:
        copy.wait()


def finish_kernel(txe, tye, tze, basis, xh, zh, c4, acc, rhs, pressure_out, residual_out,
                  tx_s, ty_s, tz_s, g_s, p_s, sem_in):
    loads = []
    for t in range(NT):
        lanes = pl.ds(128 * t, 128)
        for k, (hbm, vmem) in enumerate(((txe.at[pl.ds(4, 17)], tx_s), (tye.at[pl.ds(4, 16)], ty_s),
                                         (tze.at[pl.ds(4, 16)], tz_s))):
            copy = pltpu.make_async_copy(hbm.at[:, pl.ds(0, 24), lanes], vmem.at[:, t], sem_in.at[k * NT + t])
            copy.start()
            loads.append(copy)
    sub = iota((8, 128), 0)
    lane = iota((8, 128), 1)
    upper = sub >= 4

    j, y = iota((128, 512), 0), iota((128, 512), 1)
    block = y // 8
    side = jnp.where(y % 8 >= 4, 1, -1)
    spread = []
    for d in range(2):
        node = jnp.where(block % 2 == d, block, block + side)
        spread.append(jnp.dot(c4[...], (j == node).astype(F32), precision=lax.Precision.HIGHEST,
                              preferred_element_type=F32))
    for nx in range(4):
        for c in range(2):
            for d in range(2):
                def row(nz):
                    return spread[d][nz * 8 + nx + 1:nz * 8 + nx + 2, :]
                if c == 0:
                    tiles = (row(1), row(1)), (row(1), row(3))
                else:
                    tiles = (row(0), row(2)), (row(2), row(2))
                for zb in range(2):
                    for t in range(NT):
                        a, b = (jnp.broadcast_to(v[:, 128 * t:128 * t + 128], (8, 128)) for v in tiles[zb])
                        g_s[nx, 2 * c + d, t, 8 * zb:8 * zb + 8, :] = jnp.where(upper, b, a)

    def plane_nodes(X):
        block_x = (X + 4) // 8 - 1
        par = (block_x + 2) % 2
        up = (X + 4) % 8 >= 4
        flip = block_x + 1 + jnp.where(up, 1, -1)
        own = block_x + 1
        return jnp.where(par == 0, own, flip), jnp.where(par == 0, flip, own)

    def prolong(read, X, t, zb):
        n0, n1 = plane_nodes(X)
        total = None
        for s in range(8):
            n = n0 if s < 4 else n1
            term = read(s) * g_s[n, s % 4, t, 8 * zb:8 * zb + 8, :]
            total = term if total is None else total + term
        return total

    def pressures(index, carry):
        x, t = index // NT, index % NT
        lanes = pl.ds(pl.multiple_of(t * 128, 128), 128)
        for zb in range(2):
            p = prolong(lambda s: basis[s, x, 8 * zb:8 * zb + 8, lanes], x + 4, t, zb)
            p_s[x + 1, t, 8 + 8 * zb:16 + 8 * zb, :] = p
            pressure_out[x, 8 * zb:8 * zb + 8, lanes] = p
        return carry

    lax.fori_loop(0, 16 * NT, pressures, 0)

    def outer(t, carry):
        lanes = pl.ds(pl.multiple_of(t * 128, 128), 128)
        for zb in range(2):
            for s_x, X, at in ((0, 3, 0), (1, 20, 17)):
                p = prolong(lambda s: xh[s, s_x, 8 * zb:8 * zb + 8, lanes], X, t, zb)
                p_s[at, t, 8 + 8 * zb:16 + 8 * zb, :] = p
        return carry

    lax.fori_loop(0, NT, outer, 0)
    flat = p_s.reshape(18 * NT * NR, 128)
    for t in range(NT):
        cols = slice(128 * t, 128 * t + 128)
        for s_z, R in ((0, 7), (1, 24)):
            for half in range(2):
                total = None
                for s in range(8):
                    a, c, d = s // 4, (s // 2) % 2, s % 2
                    nz = (1, 0)[c] if s_z == 0 else (3, 2)[c]
                    def row(nx):
                        return jnp.broadcast_to(spread[d][nz * 8 + nx + 1:nz * 8 + nx + 2, cols], (8, 128))
                    if a == 0:
                        value = row(1) if half == 0 else jnp.where(upper, row(3), row(1))
                    else:
                        value = jnp.where(upper, row(2), row(0)) if half == 0 else row(2)
                    term = zh[s, s_z, 8 * half:8 * half + 8, cols] * value
                    total = term if total is None else total + term
                flat[pl.ds(((1 + 8 * half) * NT + t) * NR + R, 8, stride=NT * NR), :] = total
    for copy in loads:
        copy.wait()

    def to_prev(value, left):
        return roll(jnp.where(lane == 127, left, value), 1)

    def to_next(value, right):
        return roll(jnp.where(lane == 0, right, value), 127)

    def residuals(index, carry):
        x, t = index // NT, index % NT
        lanes = pl.ds(pl.multiple_of(t * 128, 128), 128)
        tl, tr = jnp.maximum(t - 1, 0), jnp.minimum(t + 1, NT - 1)
        for zb in range(2):
            R = 8 + 8 * zb
            rows = pl.ds(R, 8)
            p = p_s[x + 1, t, rows, :]
            ty = ty_s[x, t, rows, :]
            tym = jnp.where((lane == 0) & (t == 0), 0.0, to_prev(ty, ty_s[x, tl, rows, :]))
            flow = acc[x, 8 * zb:8 * zb + 8, lanes] * p
            flow += tx_s[x + 1, t, rows, :] * (p - p_s[x + 2, t, rows, :])
            flow += tx_s[x, t, rows, :] * (p - p_s[x, t, rows, :])
            flow += tz_s[x, t, rows, :] * (p - p_s[x + 1, t, pl.ds(R + 1, 8), :])
            flow += tz_s[x, t, pl.ds(R - 1, 8), :] * (p - p_s[x + 1, t, pl.ds(R - 1, 8), :])
            flow += ty * (p - to_next(p, p_s[x + 1, tr, rows, :]))
            flow += tym * (p - to_prev(p, p_s[x + 1, tl, rows, :]))
            residual_out[x, 8 * zb:8 * zb + 8, lanes] = rhs[x, 8 * zb:8 * zb + 8, lanes] - flow
        return carry

    lax.fori_loop(0, 16 * NT, residuals, 0)


VMEM_SPEC = pl.BlockSpec(memory_space=pltpu.VMEM)
SMEM_SPEC = pl.BlockSpec(memory_space=pltpu.SMEM)
ANY_SPEC = pl.BlockSpec(memory_space=pl.ANY)


def run_main(txe, tye, tze, acc, src, wcell, wrate):
    field = pltpu.VMEM((NXE, NT, NR, 128), F32)
    return pl.pallas_call(
        main_kernel,
        name="sweeps",
        out_shape=(jax.ShapeDtypeStruct((8, 16, 16, 512), F32), jax.ShapeDtypeStruct((2, 32, 128), F32),
                   jax.ShapeDtypeStruct((16, 16, 512), F32), jax.ShapeDtypeStruct((8, 2, 16, 512), F32),
                   jax.ShapeDtypeStruct((8, 2, 16, 512), F32)),
        in_specs=[ANY_SPEC] * 3 + [VMEM_SPEC] * 2 + [SMEM_SPEC] * 2,
        out_specs=(ANY_SPEC, VMEM_SPEC, VMEM_SPEC, ANY_SPEC, VMEM_SPEC),
        scratch_shapes=[
            pltpu.VMEM((NXE + 1, NT, NR, 128), F32), field, field, field, field,
            pltpu.VMEM((8, NXE, NT, NR, 128), F32), pltpu.VMEM((8, NXE, NT, NR, 128), F32),
            pltpu.VMEM((NT, 448, 128), F32),
            pltpu.SemaphoreType.DMA((3 * NT,)), pltpu.SemaphoreType.DMA((8 * NT,)),
            pltpu.SemaphoreType.DMA((16 * NT,)),
        ],
        compiler_params=pltpu.CompilerParams(vmem_limit_bytes=60 * 1024 * 1024),
        interpret=INTERPRET,
    )(txe, tye, tze, acc, src, wcell, wrate)


def run_finish(txe, tye, tze, basis, xh, zh, c4, acc, rhs):
    return pl.pallas_call(
        finish_kernel,
        name="finish",
        out_shape=(jax.ShapeDtypeStruct((16, 16, 512), F32), jax.ShapeDtypeStruct((16, 16, 512), F32)),
        in_specs=[ANY_SPEC] * 3 + [VMEM_SPEC] * 6,
        out_specs=(VMEM_SPEC, VMEM_SPEC),
        scratch_shapes=[
            pltpu.VMEM((17, NT, 24, 128), F32), pltpu.VMEM((16, NT, 24, 128), F32), pltpu.VMEM((16, NT, 24, 128), F32),
            pltpu.VMEM((4, 4, NT, 16, 128), F32), pltpu.VMEM((18, NT, NR, 128), F32),
            pltpu.SemaphoreType.DMA((3 * NT,)),
        ],
        compiler_params=pltpu.CompilerParams(vmem_limit_bytes=60 * 1024 * 1024),
        interpret=INTERPRET,
    )(txe, tye, tze, basis, xh, zh, c4, acc, rhs)


NEAR = [(dt, dg) for dt in (-1, 0, 1) for dg in (-1, 0, 1) if (dt, dg) != (0, 0)]


def slot_of(dt, dg):
    return (dt + 1) * 3 + dg + 1


def neighbours():
    tile, gz = lax.axis_index("tile"), lax.axis_index("gz")
    tiles, layers = lax.axis_size("tile"), lax.axis_size("gz")
    found = []
    for dt, dg in NEAR:
        here = (tile + dt >= 0) & (tile + dt < tiles) & (gz + dg >= 0) & (gz + dg < layers)
        found.append((dt, dg, here, (tile + dt, gz + dg)))
    return found


def greet(near):
    barrier = pltpu.get_barrier_semaphore()
    count = 0
    for dt, dg, here, device in near:
        @pl.when(here)
        def _():
            pl.semaphore_signal(barrier, inc=1, device_id=device, device_id_type=pl.DeviceIdType.MESH)
        count = count + here.astype(jnp.int32)
    pl.semaphore_wait(barrier, count)


def coarse_kernel(packed, c_out, ops, got, mine, op_send, op_recv, c_send, c_recv):
    near = neighbours()
    ops[...] = jnp.zeros(ops.shape, F32)
    got[...] = jnp.zeros(got.shape, F32)
    greet(near)

    def op_copies(dt, dg, device):
        made = []
        for n, xb in enumerate({1: (1,), -1: (0,), 0: (0, 1)}[dt]):
            made.append(pltpu.make_async_remote_copy(
                src_ref=packed.at[xb], dst_ref=ops.at[2 * (1 - dt) + xb, 1 - dg],
                send_sem=op_send.at[slot_of(dt, dg), n], recv_sem=op_recv.at[slot_of(-dt, -dg), n],
                device_id=device, device_id_type=pl.DeviceIdType.MESH))
        return made

    def c_copy(r, dt, dg, device):
        return pltpu.make_async_remote_copy(
            src_ref=mine.at[r], dst_ref=got.at[r, slot_of(-dt, -dg)],
            send_sem=c_send.at[r, slot_of(dt, dg)], recv_sem=c_recv.at[r, slot_of(-dt, -dg)],
            device_id=device, device_id_type=pl.DeviceIdType.MESH)

    def each(act):
        for dt, dg, here, device in near:
            @pl.when(here)
            def _():
                act(dt, dg, device)

    def send(r):
        each(lambda dt, dg, device: c_copy(r, dt, dg, device).start())

    def arrive(r):
        each(lambda dt, dg, device: c_copy(r, -dt, -dg, device).wait_recv())

    for xb in range(2):
        mine[0, xb:xb + 1, :] = COARSE_STEP * packed[xb, 27:28, :] / packed[xb, 28:29, :]
        ops[2 + xb, 1] = packed[xb]
    send(0)
    each(lambda dt, dg, device: [c.start() for c in op_copies(dt, dg, device)])

    lane = iota((8, 128), 1)
    row = iota((8, 128), 0)
    table = ops.reshape(8 * 3 * 32, 128)

    def entry(g, k):
        return table[pl.ds(g * 32 + k, 8, stride=96), :]

    def gather(r):
        fields = []
        for g in range(3):
            parts = []
            for dt in (-1, 0, 1):
                parts.append(mine[r, 0:2, :] if (dt, g) == (0, 1) else got[r, slot_of(dt, g - 1), 0:2, :])
            fields.append(jnp.concatenate(parts + [jnp.zeros((2, 128), F32)], 0))
        return fields

    def lanes_from(fields, g, by):
        if by == 0:
            return fields[g]
        if by > 0:
            after = fields[min(g + 1, 2)]
            return jnp.where(lane < 128 - by, roll(fields[g], 128 - by), roll(after, 128 - by))
        before = fields[max(g - 1, 0)]
        return jnp.where(lane >= -by, roll(fields[g], -by), roll(before, -by))

    def iterate(fields):
        totals = [None] * 3
        for dx in (-1, 0, 1):
            moved = fields if dx == 0 else [pltpu.roll(f, 1 if dx == -1 else 7, 0) for f in fields]
            for dz in (-1, 0, 1):
                for dy in (-1, 0, 1):
                    k = (dx + 1) * 9 + (dz + 1) * 3 + dy + 1
                    for g in range(3):
                        term = entry(g, k) * lanes_from(moved, g, 64 * dz + dy)
                        totals[g] = term if totals[g] is None else totals[g] + term
        result = []
        for g in range(3):
            scale = entry(g, 28)
            safe = jnp.where(scale > 0.0, scale, 1.0)
            value = fields[g] + COARSE_STEP * (entry(g, 27) - totals[g]) / safe
            result.append(jnp.where(scale > 0.0, value, 0.0))
        return result

    arrive(0)
    each(lambda dt, dg, device: [c.wait_recv() for c in op_copies(-dt, -dg, device)])
    for r in range(3):
        if r:
            arrive(r)
        fields = iterate(gather(r))
        if r < 2:
            fields = iterate(fields)
            mine[r + 1, 0:2, :] = fields[1][2:4]
            send(r + 1)
    c_out[0:8, :] = roll(fields[0], 64)
    c_out[8:16, :] = fields[1]
    c_out[16:24, :] = roll(fields[1], 64)
    c_out[24:32, :] = fields[2]

    def drain(dt, dg, device):
        for copy in op_copies(dt, dg, device):
            copy.wait_send()
        for r in range(3):
            c_copy(r, dt, dg, device).wait_send()

    each(drain)


def run_coarse(packed):
    return pl.pallas_call(
        coarse_kernel,
        name="coarse",
        out_shape=jax.ShapeDtypeStruct((32, 128), F32),
        in_specs=[VMEM_SPEC],
        out_specs=VMEM_SPEC,
        scratch_shapes=[
            pltpu.VMEM((8, 3, 32, 128), F32), pltpu.VMEM((3, 9, 8, 128), F32), pltpu.VMEM((3, 8, 128), F32),
            pltpu.SemaphoreType.DMA((9, 2)), pltpu.SemaphoreType.DMA((9, 2)),
            pltpu.SemaphoreType.DMA((3, 9)), pltpu.SemaphoreType.DMA((3, 9)),
        ],
        compiler_params=pltpu.CompilerParams(collective_id=1, has_side_effects=True),
        interpret=COMM_INTERPRET,
    )(packed)


def shift_up(value, axis):
    size = lax.axis_size(axis)
    return lax.ppermute(value, axis, [(i, i + 1) for i in range(size - 1)])


def shift_down(value, axis):
    size = lax.axis_size(axis)
    return lax.ppermute(value, axis, [(i + 1, i) for i in range(size - 1)])


def extend(tx, ty, tz):
    up = jnp.concatenate([tx[:, 12:], ty[:, 12:], tz[:, 11:]], 1)
    down = jnp.concatenate([tx[:, :4], ty[:, :4], tz[:, :4]], 1)
    low, high = shift_up(up, "gz"), shift_down(down, "gz")
    fill = jnp.zeros((16, 4, 512), F32)
    txz = jnp.concatenate([low[:, :4], tx, high[:, :4]], 1)
    tyz = jnp.concatenate([low[:, 4:8], ty, high[:, 4:8]], 1)
    tzz = jnp.concatenate([low[:, 9:13], tz, high[:, 8:12]], 1)
    up = jnp.concatenate([txz[11:], tyz[12:], tzz[12:]], 0)
    down = jnp.concatenate([txz[:4], tyz[:4], tzz[:4]], 0)
    lowx, highx = shift_up(up, "tile"), shift_down(down, "tile")
    txe = jnp.pad(jnp.concatenate([lowx[:5], txz, highx[:4]], 0), ((0, 0), (4, 4), (0, 0)))
    tye = jnp.pad(jnp.concatenate([lowx[5:9], tyz, highx[4:8]], 0), ((0, 0), (4, 4), (0, 0)))
    tze = jnp.pad(jnp.concatenate([lowx[9:13], tzz, highx[8:12]], 0), ((0, 0), (4, 4), (0, 0)))
    extra = jnp.pad(low[:, 8:9], ((4, 4), (3, 28), (0, 0)))
    return txe, tye, tze + extra


def body(trans_x, trans_y, trans_z, accumulation, source, well_cell, well_rate):
    last_x = lax.axis_index("tile") == lax.axis_size("tile") - 1
    last_z = lax.axis_index("gz") == lax.axis_size("gz") - 1
    tx = jnp.where((jnp.arange(16) == 15)[:, None, None] & last_x, 0.0, trans_x)
    tz = jnp.where((jnp.arange(16) == 15)[None, :, None] & last_z, 0.0, trans_z)
    ty = jnp.where((jnp.arange(512) == 511)[None, None, :], 0.0, trans_y)
    txe, tye, tze = extend(tx, ty, tz)
    basis, packed, rhs, xh, zh = run_main(txe, tye, tze, accumulation, source, well_cell, well_rate)
    c4 = run_coarse(packed)
    pressure, residual = run_finish(txe, tye, tze, basis, xh, zh, c4, accumulation, rhs)
    return basis, pressure, residual


def solution(mesh):
    grid = P("tile", "gz", None)
    return jax.shard_map(
        body,
        mesh=mesh,
        in_specs=(grid,) * 5 + (P("tile", "gz"),) * 2,
        out_specs=(P(None, "tile", "gz", None), grid, grid),
        check_vma=False,
    )
```

```python
import jax
import jax.numpy as jnp
from jax import lax
from jax.experimental import pallas as pl
from jax.experimental.pallas import tpu as pltpu
from jax.sharding import PartitionSpec as P

COARSE_STEP = 0.5
NT = 4
NXE = 24
NR = 32
F32 = jnp.float32
INTERPRET = False
COMM_INTERPRET = False


def iota(shape, dim):
    return lax.broadcasted_iota(jnp.int32, shape, dim)


def roll(value, shift):
    return pltpu.roll(value, shift, 1)


def select_dot(table, value):
    total = None
    for _ in range(3):
        part = value.astype(jnp.bfloat16)
        value = value - part.astype(F32)
        term = jnp.dot(*table(part), preferred_element_type=F32)
        total = term if total is None else total + term
    return total


LO_SPANS = (4, 4, 5)
HI_SPANS = (4, 4, 4)
ZROWS = 216


def z_row(x):
    return 13 * x + 4 * (x >= 4)


def main_kernel(tx_in, ty_in, tz_in, xlo, xhi, zlo, zhi, corners, acc, src, wcell, wrate,
                basis_out, coarse_out, rhs_out, xh_out, zh_out,
                tx_s, ty_s, tz_s, tym_s, dd_s, b0, b1, sums, sem_in, sem_out, sem_x):
    loads = []
    pieces = ((tx_in, 0, 16, tx_s, 5), (xlo, 0, 5, tx_s, 0), (xhi, 0, 4, tx_s, 21),
              (ty_in, 0, 16, ty_s, 4), (xlo, 5, 4, ty_s, 0), (xhi, 4, 4, ty_s, 20),
              (tz_in, 0, 16, tz_s, 4), (xlo, 9, 4, tz_s, 0), (xhi, 8, 4, tz_s, 20))
    for t in range(NT):
        for k, (hbm, first_in, count, vmem, first_out) in enumerate(pieces):
            copy = pltpu.make_async_copy(hbm.at[pl.ds(first_in, count), :, pl.ds(128 * t, 128)],
                                         vmem.at[pl.ds(first_out, count), t, pl.ds(8, 16), :],
                                         sem_in.at[k * NT + t])
            copy.start()
            loads.append(copy)
    for x in range(-4, 20):
        for side, top, spans in ((0, 4, LO_SPANS), (1, 24, HI_SPANS)):
            for t in range(NT):
                if 0 <= x < 16:
                    piece, base = (zlo, zhi)[side], z_row(x)
                else:
                    piece, base = corners.at[2 * (x >= 16) + side], 13 * (x % 16) - 156 * (x < 0)
                for at, count, ref, shift in zip((0, 4, 8), spans, (tx_s, ty_s, tz_s), (5, 4, 4)):
                    row = top - (count - 4)
                    ref[x + shift, t, row:row + count, :] = piece[t, base + at:base + at + count, :]
    rhs_out[...] = src[...]
    lane_y = iota((1, 512), 1)
    for w in range(16):
        cell = wcell[w, 0]
        row = cell // 512
        x, z, y = row // 16, row % 16, cell % 512
        old = rhs_out[x, pl.ds(z, 1), :]
        rhs_out[x, pl.ds(z, 1), :] = old + jnp.where(lane_y == y, wrate[w, 0], 0.0)
    for copy in loads:
        copy.wait()

    @pl.when(lax.axis_index("tile") == lax.axis_size("tile") - 1)
    def _():
        for t in range(NT):
            tx_s[20, t, 0:32, :] = jnp.zeros((NR, 128), F32)

    @pl.when(lax.axis_index("gz") == lax.axis_size("gz") - 1)
    def _():
        for X in range(NXE):
            for t in range(NT):
                tz_s[X, t, 23:24, :] = jnp.zeros((1, 128), F32)

    sub = iota((8, 128), 0)
    lane = iota((8, 128), 1)
    yo = lane % 8
    lane_par = (lane // 8) % 2
    zero = jnp.zeros((8, 128), F32)

    def to_prev(value, left):
        return roll(jnp.where(lane == 127, left, value), 1)

    def to_next(value, right):
        return roll(jnp.where(lane == 0, right, value), 127)

    def first(X, carry):
        for t in range(NT):
            first_tile(X, t)
        return carry

    def first_tile(X, t):
        tl = max(t - 1, 0)
        par = ((X + 4) // 8 + 1) % 2
        xo = (X + 4) % 8
        own_base, flip_base = par * 4, 4 - par * 4
        lo_x = (xo == 0).astype(F32)
        hi_x = (xo == 7).astype(F32)
        for r in range(3):
            R = 4 + 8 * r
            rows = pl.ds(R, 8)
            tx, txm = tx_s[X + 1, t, rows, :], tx_s[X, t, rows, :]
            tz, tzm = tz_s[X, t, rows, :], tz_s[X, t, pl.ds(R - 1, 8), :]
            ty = ty_s[X, t, rows, :]
            if t == NT - 1:
                ty = jnp.where(lane == 127, 0.0, ty)
                ty_s[X, t, rows, :] = ty
            tym = to_prev(ty, ty_s[X, tl, rows, :])
            if t == 0:
                tym = jnp.where(lane == 0, 0.0, tym)
            diag = tx + txm + tz + tzm + ty + tym
            half = diag * 0.5 + 1e-30
            tym_s[X, t, rows, :] = tym
            dd_s[X, t, rows, :] = half
            txb = lo_x * txm + hi_x * tx
            tzb = jnp.where(sub == 3, tz, jnp.where(sub == 4, tzm, 0.0))
            tyb = jnp.where(yo == 7, ty, jnp.where(yo == 0, tym, 0.0))
            own = half + (diag - txb - tzb - tyb)
            inv = 1.0 / (own + txb + tzb + tyb)
            own, vx, vz, vy = own * inv, txb * inv, tzb * inv, tyb * inv
            row_par = jnp.where(sub < 4, (r + 1) % 2, r % 2)
            for c in range(2):
                for d in range(2):
                    in_row, in_lane = row_par == c, lane_par == d
                    value = jnp.where(in_row, jnp.where(in_lane, own, vy), jnp.where(in_lane, vz, 0.0))
                    b0[own_base + 2 * c + d, X, t, rows, :] = value
                    b0[flip_base + 2 * c + d, X, t, rows, :] = jnp.where(in_row & in_lane, vx, 0.0)
                    b1[flip_base + 2 * c + d, X, t, rows, :] = zero

    lax.fori_loop(0, NXE, first, 0)

    def sweep(old, new, k):
        reach = min(k, 3)

        def block(X, t, n_slots, par):
            tl, tr = max(t - 1, 0), min(t + 1, NT - 1)
            own_base, flip_base = par * 4, 4 - par * 4
            for r in range(3):
                R = 4 + 8 * r
                rows = pl.ds(R, 8)
                tx, txm = tx_s[X + 1, t, rows, :], tx_s[X, t, rows, :]
                tz, tzm = tz_s[X, t, rows, :], tz_s[X, t, pl.ds(R - 1, 8), :]
                ty, tym = ty_s[X, t, rows, :], tym_s[X, t, rows, :]
                half = dd_s[X, t, rows, :]
                row_par = jnp.where(sub < 4, (r + 1) % 2, r % 2)
                values = []
                for cd in range(n_slots):
                    c, d = (cd // 2) % 2, cd % 2
                    s = (own_base if cd < 4 else flip_base) + cd % 4
                    b = old[s, X, t, rows, :]
                    v = half * b
                    v += tx * old[s, X + 1, t, rows, :]
                    v += txm * old[s, X - 1, t, rows, :]
                    v += tz * old[s, X, t, pl.ds(R + 1, 8), :]
                    v += tzm * old[s, X, t, pl.ds(R - 1, 8), :]
                    v += ty * to_next(b, old[s, X, tr, rows, :])
                    v += tym * to_prev(b, old[s, X, tl, rows, :])
                    if k == 4:
                        out_z = (row_par != c) & ((sub == 0) | (sub == 7))
                        out_y = (lane_par != d) & ((yo == 3) | (yo == 4))
                        v = jnp.where(out_z | out_y, 0.0, v)
                    values.append(v)
                total = values[0]
                for v in values[1:]:
                    total = total + v
                inv = 1.0 / total
                for cd in range(n_slots):
                    s = (own_base if cd < 4 else flip_base) + cd % 4
                    new[s, X, t, rows, :] = values[cd] * inv

        def step(X, carry):
            par = ((X + 4) // 8 + 1) % 2
            xo = (X + 4) % 8
            dist = jnp.where(xo < 4, xo + 1, 8 - xo)

            @pl.when(dist <= reach)
            def _():
                for t in range(NT):
                    block(X, t, 8, par)

            @pl.when(dist > reach)
            def _():
                for t in range(NT):
                    block(X, t, 4, par)

            return carry

        lax.fori_loop(k - 1, 25 - k, step, 0)

    sweep(b0, b1, 2)
    sweep(b1, b0, 3)
    sweep(b0, b1, 4)

    stores = []
    for s in range(8):
        for t in range(NT):
            copy = pltpu.make_async_copy(b1.at[s, pl.ds(4, 16), t, pl.ds(8, 16), :],
                                         basis_out.at[s, :, :, pl.ds(128 * t, 128)], sem_out.at[s * NT + t])
            copy.start()
            stores.append(copy)
            for side, X in enumerate((3, 20)):
                copy = pltpu.make_async_copy(b1.at[s, X, t, pl.ds(8, 16), :],
                                             xh_out.at[s, side, :, pl.ds(128 * t, 128)],
                                             sem_x.at[(s * NT + t) * 2 + side])
                copy.start()
                stores.append(copy)

    flat = b1.reshape(8 * NXE * NT * NR, 128)

    def rows_of(index, carry):
        s, t = index // NT, index % NT
        lanes = pl.ds(pl.multiple_of(t * 128, 128), 128)
        for side, R in enumerate((7, 24)):
            for half in range(2):
                start = ((s * NXE + 4 + 8 * half) * NT + t) * NR + R
                zh_out[s, side, 8 * half:8 * half + 8, lanes] = flat[pl.ds(start, 8, stride=NT * NR), :]
        return carry

    lax.fori_loop(0, 8 * NT, rows_of, 0)

    for zb in range(2):
        R = 8 + 8 * zb

        def edges(index, carry):
            xb, t = index // NT, index % NT
            tl, tr = jnp.maximum(t - 1, 0), jnp.minimum(t + 1, NT - 1)
            rows = pl.ds(R, 8)
            lanes = pl.ds(pl.multiple_of(t * 128, 128), 128)
            own_base, flip_base = xb * 4, 4 - xb * 4
            groups = [[None] * 4 for _ in range(3)]
            scale = zero
            right = zero
            for xo in range(8):
                X = 4 + xb * 8 + xo
                x = xb * 8 + xo
                tz, tzm = tz_s[X, t, rows, :], tz_s[X, t, pl.ds(R - 1, 8), :]
                ty, tym = ty_s[X, t, rows, :], tym_s[X, t, rows, :]
                tzb = jnp.where(sub == 7, tz, jnp.where(sub == 0, tzm, 0.0))
                tyb = jnp.where(yo == 7, ty, jnp.where(yo == 0, tym, 0.0))
                central = acc[x, 8 * zb:8 * zb + 8, lanes] + tzb + tyb
                if xo == 0:
                    txb, xn = tx_s[X, t, rows, :], X - 1
                    central = central + txb
                if xo == 7:
                    txb, xn = tx_s[X + 1, t, rows, :], X + 1
                    central = central + txb
                scale = scale + central
                right = right + rhs_out[x, 8 * zb:8 * zb + 8, lanes]
                which = [(0, own_base)]
                if xo < 3:
                    which.append((1, flip_base))
                if xo > 4:
                    which.append((2, flip_base))
                for g, base in which:
                    for cd in range(4):
                        s = base + cd
                        b = b1[s, X, t, rows, :]
                        bz = jnp.where(sub == 7, b1[s, X, t, pl.ds(R + 1, 8), :], b1[s, X, t, pl.ds(R - 1, 8), :])
                        by = jnp.where(yo == 7, to_next(b, b1[s, X, tr, rows, :]), to_prev(b, b1[s, X, tl, rows, :]))
                        e = central * b - tzb * bz - tyb * by
                        if xo in (0, 7):
                            e = e - txb * b1[s, xn, t, rows, :]
                        groups[g][cd] = e if groups[g][cd] is None else groups[g][cd] + e
            for g in range(3):
                for cd in range(4):
                    u = xb * 12 + g * 4 + cd
                    sums[t, pl.ds(pl.multiple_of(u * 16 + 8 * zb, 8), 8), :] = groups[g][cd]
            sums[t, pl.ds(pl.multiple_of((24 + xb) * 16 + 8 * zb, 8), 8), :] = scale
            sums[t, pl.ds(pl.multiple_of((26 + xb) * 16 + 8 * zb, 8), 8), :] = right
            return carry

        lax.fori_loop(0, 2 * NT, edges, 0)

    l_y, l_j = iota((128, 128), 0), iota((128, 128), 1)
    folded = jnp.zeros((448, 128), F32)
    for t in range(NT):
        target = ((l_y % 8) // 4) * 64 + 16 * t + l_y // 8
        chosen = (l_j == target).astype(jnp.bfloat16)
        folded = folded + select_dot(lambda part: (part, chosen), sums[t])
    o, i = iota((128, 448), 0), iota((128, 448), 1)
    pick = ((i // 16 == o % 32) & ((i % 16) // 4 == o // 32)).astype(jnp.bfloat16)
    quarters = select_dot(lambda part: (pick, part), folded)

    lane1 = iota((1, 128), 1)
    odd = lane1 % 2 == 1
    low = lane1 < 64

    def unit(q, u):
        return quarters[q * 32 + u:q * 32 + u + 1, :]

    def halves(value):
        return value + roll(value, 64)

    for xb in range(2):
        for dx, g in ((0, 1), (1, 0), (2, 2)):
            for dz in range(3):
                parts = []
                for zb in range(2):
                    c = zb if dz == 1 else 1 - zb
                    vs = []
                    for d in range(2):
                        u = xb * 12 + g * 4 + c * 2 + d
                        if dz == 0:
                            vs.append(unit(2 * zb, u))
                        elif dz == 2:
                            vs.append(unit(2 * zb + 1, u))
                        else:
                            vs.append(unit(2 * zb, u) + unit(2 * zb + 1, u))
                    own = jnp.where(odd, vs[1], vs[0])
                    flip = jnp.where(odd, vs[0], vs[1])
                    turned = roll(flip, 64)
                    parts.append((flip, halves(own), turned) if zb == 0 else (turned, halves(own), flip))
                for dy in range(3):
                    k = dx * 9 + dz * 3 + dy
                    coarse_out[xb, k:k + 1, :] = jnp.where(low, parts[0][dy], parts[1][dy])
        for k, u in ((27, 26 + xb), (28, 24 + xb)):
            parts = [halves(unit(2 * zb, u) + unit(2 * zb + 1, u)) for zb in range(2)]
            coarse_out[xb, k:k + 1, :] = jnp.where(low, parts[0], parts[1])
        coarse_out[xb, 29:32, :] = jnp.zeros((3, 128), F32)

    for copy in stores:
        copy.wait()


def finish_kernel(tx_in, ty_in, tz_in, xlo, zlo, basis, xh, zh, c4, acc, rhs, pressure_out, residual_out,
                  tx_s, ty_s, tz_s, g_s, p_s, sem_in):
    loads = []
    pieces = ((tx_in, 0, 16, tx_s, 1), (xlo, 4, 1, tx_s, 0), (ty_in, 0, 16, ty_s, 0), (tz_in, 0, 16, tz_s, 0))
    for t in range(NT):
        for k, (hbm, first_in, count, vmem, first_out) in enumerate(pieces):
            copy = pltpu.make_async_copy(hbm.at[pl.ds(first_in, count), :, pl.ds(128 * t, 128)],
                                         vmem.at[pl.ds(first_out, count), t, pl.ds(8, 16), :],
                                         sem_in.at[k * NT + t])
            copy.start()
            loads.append(copy)
        for x in range(16):
            tz_s[x, t, 7:8, :] = zlo[t, z_row(x) + 12:z_row(x) + 13, :]
    sub = iota((8, 128), 0)
    lane = iota((8, 128), 1)
    upper = sub >= 4

    j, y = iota((128, 512), 0), iota((128, 512), 1)
    block = y // 8
    side = jnp.where(y % 8 >= 4, 1, -1)
    spread = []
    for d in range(2):
        node = jnp.where(block % 2 == d, block, block + side)
        chosen = (j == node).astype(jnp.bfloat16)
        spread.append(select_dot(lambda part: (part, chosen), c4[...]))
    for nx in range(4):
        for c in range(2):
            for d in range(2):
                def row(nz):
                    return spread[d][nz * 8 + nx + 1:nz * 8 + nx + 2, :]
                if c == 0:
                    tiles = (row(1), row(1)), (row(1), row(3))
                else:
                    tiles = (row(0), row(2)), (row(2), row(2))
                for zb in range(2):
                    for t in range(NT):
                        a, b = (jnp.broadcast_to(v[:, 128 * t:128 * t + 128], (8, 128)) for v in tiles[zb])
                        g_s[nx, 2 * c + d, t, 8 * zb:8 * zb + 8, :] = jnp.where(upper, b, a)

    def plane_nodes(X):
        block_x = (X + 4) // 8 - 1
        par = (block_x + 2) % 2
        up = (X + 4) % 8 >= 4
        flip = block_x + 1 + jnp.where(up, 1, -1)
        own = block_x + 1
        return jnp.where(par == 0, own, flip), jnp.where(par == 0, flip, own)

    def prolong(read, X, t, zb):
        n0, n1 = plane_nodes(X)
        total = None
        for s in range(8):
            n = n0 if s < 4 else n1
            term = read(s) * g_s[n, s % 4, t, 8 * zb:8 * zb + 8, :]
            total = term if total is None else total + term
        return total

    def pressures(x, carry):
        for t in range(NT):
            lanes = pl.ds(t * 128, 128)
            for zb in range(2):
                p = prolong(lambda s: basis[s, x, 8 * zb:8 * zb + 8, lanes], x + 4, t, zb)
                p_s[x + 1, t, 8 + 8 * zb:16 + 8 * zb, :] = p
                pressure_out[x, 8 * zb:8 * zb + 8, lanes] = p
        return carry

    lax.fori_loop(0, 16, pressures, 0)

    def outer(t, carry):
        lanes = pl.ds(pl.multiple_of(t * 128, 128), 128)
        for zb in range(2):
            for s_x, X, at in ((0, 3, 0), (1, 20, 17)):
                p = prolong(lambda s: xh[s, s_x, 8 * zb:8 * zb + 8, lanes], X, t, zb)
                p_s[at, t, 8 + 8 * zb:16 + 8 * zb, :] = p
        return carry

    lax.fori_loop(0, NT, outer, 0)
    flat = p_s.reshape(18 * NT * NR, 128)
    for t in range(NT):
        cols = slice(128 * t, 128 * t + 128)
        for s_z, R in ((0, 7), (1, 24)):
            for half in range(2):
                total = None
                for s in range(8):
                    a, c, d = s // 4, (s // 2) % 2, s % 2
                    nz = (1, 0)[c] if s_z == 0 else (3, 2)[c]
                    def row(nx):
                        return jnp.broadcast_to(spread[d][nz * 8 + nx + 1:nz * 8 + nx + 2, cols], (8, 128))
                    if a == 0:
                        value = row(1) if half == 0 else jnp.where(upper, row(3), row(1))
                    else:
                        value = jnp.where(upper, row(2), row(0)) if half == 0 else row(2)
                    term = zh[s, s_z, 8 * half:8 * half + 8, cols] * value
                    total = term if total is None else total + term
                flat[pl.ds(((1 + 8 * half) * NT + t) * NR + R, 8, stride=NT * NR), :] = total
    for copy in loads:
        copy.wait()

    @pl.when(lax.axis_index("tile") == lax.axis_size("tile") - 1)
    def _():
        for t in range(NT):
            tx_s[16, t, 8:24, :] = jnp.zeros((16, 128), F32)

    @pl.when(lax.axis_index("gz") == lax.axis_size("gz") - 1)
    def _():
        for x in range(16):
            for t in range(NT):
                tz_s[x, t, 23:24, :] = jnp.zeros((1, 128), F32)

    def to_prev(value, left):
        return roll(jnp.where(lane == 127, left, value), 1)

    def to_next(value, right):
        return roll(jnp.where(lane == 0, right, value), 127)

    def residuals(x, carry):
        for t in range(NT):
            lanes = pl.ds(t * 128, 128)
            tl, tr = max(t - 1, 0), min(t + 1, NT - 1)
            for zb in range(2):
                R = 8 + 8 * zb
                rows = pl.ds(R, 8)
                p = p_s[x + 1, t, rows, :]
                ty = ty_s[x, t, rows, :]
                tym = to_prev(ty, ty_s[x, tl, rows, :])
                if t == 0:
                    tym = jnp.where(lane == 0, 0.0, tym)
                if t == NT - 1:
                    ty = jnp.where(lane == 127, 0.0, ty)
                flow = acc[x, 8 * zb:8 * zb + 8, lanes] * p
                flow += tx_s[x + 1, t, rows, :] * (p - p_s[x + 2, t, rows, :])
                flow += tx_s[x, t, rows, :] * (p - p_s[x, t, rows, :])
                flow += tz_s[x, t, rows, :] * (p - p_s[x + 1, t, pl.ds(R + 1, 8), :])
                flow += tz_s[x, t, pl.ds(R - 1, 8), :] * (p - p_s[x + 1, t, pl.ds(R - 1, 8), :])
                flow += ty * (p - to_next(p, p_s[x + 1, tr, rows, :]))
                flow += tym * (p - to_prev(p, p_s[x + 1, tl, rows, :]))
                residual_out[x, 8 * zb:8 * zb + 8, lanes] = rhs[x, 8 * zb:8 * zb + 8, lanes] - flow
        return carry

    lax.fori_loop(0, 16, residuals, 0)


VMEM_SPEC = pl.BlockSpec(memory_space=pltpu.VMEM)
SMEM_SPEC = pl.BlockSpec(memory_space=pltpu.SMEM)
ANY_SPEC = pl.BlockSpec(memory_space=pl.ANY)


def run_main(tx, ty, tz, halos, acc, src, wcell, wrate):
    field = pltpu.VMEM((NXE, NT, NR, 128), F32)
    return pl.pallas_call(
        main_kernel,
        name="sweeps",
        out_shape=(jax.ShapeDtypeStruct((8, 16, 16, 512), F32), jax.ShapeDtypeStruct((2, 32, 128), F32),
                   jax.ShapeDtypeStruct((16, 16, 512), F32), jax.ShapeDtypeStruct((8, 2, 16, 512), F32),
                   jax.ShapeDtypeStruct((8, 2, 16, 512), F32)),
        in_specs=[ANY_SPEC] * 5 + [VMEM_SPEC] * 5 + [SMEM_SPEC] * 2,
        out_specs=(ANY_SPEC, VMEM_SPEC, VMEM_SPEC, ANY_SPEC, VMEM_SPEC),
        scratch_shapes=[
            pltpu.VMEM((NXE + 1, NT, NR, 128), F32), field, field, field, field,
            pltpu.VMEM((8, NXE, NT, NR, 128), F32), pltpu.VMEM((8, NXE, NT, NR, 128), F32),
            pltpu.VMEM((NT, 448, 128), F32),
            pltpu.SemaphoreType.DMA((9 * NT,)), pltpu.SemaphoreType.DMA((8 * NT,)),
            pltpu.SemaphoreType.DMA((16 * NT,)),
        ],
        compiler_params=pltpu.CompilerParams(vmem_limit_bytes=60 * 1024 * 1024),
        interpret=INTERPRET,
    )(tx, ty, tz, *halos, acc, src, wcell, wrate)


def run_finish(tx, ty, tz, xlo, zlo, basis, xh, zh, c4, acc, rhs):
    return pl.pallas_call(
        finish_kernel,
        name="finish",
        out_shape=(jax.ShapeDtypeStruct((16, 16, 512), F32), jax.ShapeDtypeStruct((16, 16, 512), F32)),
        in_specs=[ANY_SPEC] * 4 + [VMEM_SPEC] * 7,
        out_specs=(VMEM_SPEC, VMEM_SPEC),
        scratch_shapes=[
            pltpu.VMEM((17, NT, 24, 128), F32), pltpu.VMEM((16, NT, 24, 128), F32), pltpu.VMEM((16, NT, 24, 128), F32),
            pltpu.VMEM((4, 4, NT, 16, 128), F32), pltpu.VMEM((18, NT, NR, 128), F32),
            pltpu.SemaphoreType.DMA((4 * NT,)),
        ],
        compiler_params=pltpu.CompilerParams(vmem_limit_bytes=60 * 1024 * 1024),
        interpret=INTERPRET,
    )(tx, ty, tz, xlo, zlo, basis, xh, zh, c4, acc, rhs)


NEAR = [(dt, dg) for dt in (-1, 0, 1) for dg in (-1, 0, 1) if (dt, dg) != (0, 0)]


def slot_of(dt, dg):
    return (dt + 1) * 3 + dg + 1


def neighbours():
    tile, gz = lax.axis_index("tile"), lax.axis_index("gz")
    tiles, layers = lax.axis_size("tile"), lax.axis_size("gz")
    found = []
    for dt, dg in NEAR:
        here = (tile + dt >= 0) & (tile + dt < tiles) & (gz + dg >= 0) & (gz + dg < layers)
        found.append((dt, dg, here, (tile + dt, gz + dg)))
    return found


def greet(near):
    barrier = pltpu.get_barrier_semaphore()
    count = 0
    for dt, dg, here, device in near:
        @pl.when(here)
        def _():
            pl.semaphore_signal(barrier, inc=1, device_id=device, device_id_type=pl.DeviceIdType.MESH)
        count = count + here.astype(jnp.int32)
    pl.semaphore_wait(barrier, count)


def coarse_kernel(packed, c_out, table, got, mine, op_send, op_recv, c_send, c_recv):
    near = neighbours()
    table[...] = jnp.zeros(table.shape, F32)
    got[...] = jnp.zeros(got.shape, F32)
    greet(near)

    def op_copies(dt, dg, device):
        made = []
        for n, xb in enumerate({1: (1,), -1: (0,), 0: (0, 1)}[dt]):
            made.append(pltpu.make_async_remote_copy(
                src_ref=packed.at[xb], dst_ref=table.at[pl.ds(((2 * (1 - dt) + xb) * 3 + 1 - dg) * 32, 32)],
                send_sem=op_send.at[slot_of(dt, dg), n], recv_sem=op_recv.at[slot_of(-dt, -dg), n],
                device_id=device, device_id_type=pl.DeviceIdType.MESH))
        return made

    def c_copy(r, dt, dg, device):
        return pltpu.make_async_remote_copy(
            src_ref=mine.at[r], dst_ref=got.at[r, slot_of(-dt, -dg)],
            send_sem=c_send.at[r, slot_of(dt, dg)], recv_sem=c_recv.at[r, slot_of(-dt, -dg)],
            device_id=device, device_id_type=pl.DeviceIdType.MESH)

    def each(act):
        for dt, dg, here, device in near:
            @pl.when(here)
            def _():
                act(dt, dg, device)

    def send(r):
        each(lambda dt, dg, device: c_copy(r, dt, dg, device).start())

    def arrive(r):
        each(lambda dt, dg, device: c_copy(r, -dt, -dg, device).wait_recv())

    for xb in range(2):
        mine[0, xb:xb + 1, :] = COARSE_STEP * packed[xb, 27:28, :] / packed[xb, 28:29, :]
        table[((2 + xb) * 3 + 1) * 32:((2 + xb) * 3 + 2) * 32, :] = packed[xb]
    send(0)
    each(lambda dt, dg, device: [c.start() for c in op_copies(dt, dg, device)])

    lane = iota((8, 128), 1)
    row = iota((8, 128), 0)

    def entry(g, k):
        return table[pl.ds(g * 32 + k, 8, stride=96), :]

    def gather(r):
        fields = []
        for g in range(3):
            parts = []
            for dt in (-1, 0, 1):
                parts.append(mine[r, 0:2, :] if (dt, g) == (0, 1) else got[r, slot_of(dt, g - 1), 0:2, :])
            fields.append(jnp.concatenate(parts + [jnp.zeros((2, 128), F32)], 0))
        return fields

    def lanes_from(fields, g, by):
        if by == 0:
            return fields[g]
        if by > 0:
            after = fields[min(g + 1, 2)]
            return jnp.where(lane < 128 - by, roll(fields[g], 128 - by), roll(after, 128 - by))
        before = fields[max(g - 1, 0)]
        return jnp.where(lane >= -by, roll(fields[g], -by), roll(before, -by))

    def iterate(fields):
        totals = [None] * 3
        for dx in (-1, 0, 1):
            moved = fields if dx == 0 else [pltpu.roll(f, 1 if dx == -1 else 7, 0) for f in fields]
            for dz in (-1, 0, 1):
                for dy in (-1, 0, 1):
                    k = (dx + 1) * 9 + (dz + 1) * 3 + dy + 1
                    for g in range(3):
                        term = entry(g, k) * lanes_from(moved, g, 64 * dz + dy)
                        totals[g] = term if totals[g] is None else totals[g] + term
        result = []
        for g in range(3):
            scale = entry(g, 28)
            safe = jnp.where(scale > 0.0, scale, 1.0)
            value = fields[g] + COARSE_STEP * (entry(g, 27) - totals[g]) / safe
            result.append(jnp.where(scale > 0.0, value, 0.0))
        return result

    arrive(0)
    each(lambda dt, dg, device: [c.wait_recv() for c in op_copies(-dt, -dg, device)])
    for r in range(3):
        if r:
            arrive(r)
        fields = iterate(gather(r))
        if r < 2:
            fields = iterate(fields)
            mine[r + 1, 0:2, :] = fields[1][2:4]
            send(r + 1)
    c_out[0:8, :] = roll(fields[0], 64)
    c_out[8:16, :] = fields[1]
    c_out[16:24, :] = roll(fields[1], 64)
    c_out[24:32, :] = fields[2]

    def drain(dt, dg, device):
        for copy in op_copies(dt, dg, device):
            copy.wait_send()
        for r in range(3):
            c_copy(r, dt, dg, device).wait_send()

    each(drain)


def run_coarse(packed):
    return pl.pallas_call(
        coarse_kernel,
        name="coarse",
        out_shape=jax.ShapeDtypeStruct((32, 128), F32),
        in_specs=[VMEM_SPEC],
        out_specs=VMEM_SPEC,
        scratch_shapes=[
            pltpu.VMEM((8 * 3 * 32, 128), F32), pltpu.VMEM((3, 9, 8, 128), F32), pltpu.VMEM((3, 8, 128), F32),
            pltpu.SemaphoreType.DMA((9, 2)), pltpu.SemaphoreType.DMA((9, 2)),
            pltpu.SemaphoreType.DMA((3, 9)), pltpu.SemaphoreType.DMA((3, 9)),
        ],
        compiler_params=pltpu.CompilerParams(collective_id=1, has_side_effects=True),
        interpret=COMM_INTERPRET,
    )(packed)


def halo_kernel(tx, ty, tz, xlo, xhi, zlo, zhi, corners, up, down, x_send, x_recv, z_send, z_recv):
    near = neighbours()
    exists = {(dt, dg): here for dt, dg, here, _ in near}
    landing = {(-1, 0): xlo, (1, 0): xhi, (0, -1): zlo, (0, 1): zhi,
               (-1, -1): corners.at[0], (-1, 1): corners.at[1], (1, -1): corners.at[2], (1, 1): corners.at[3]}
    for where, ref in landing.items():
        @pl.when(jnp.logical_not(exists[where]))
        def _():
            ref[...] = jnp.zeros(ref.shape, F32)
    for pack, spans, ends in ((up, LO_SPANS, 16), (down, HI_SPANS, None)):
        for x in range(16):
            for at, count, ref in zip((0, 4, 8), spans, (tx, ty, tz)):
                row = 0 if ends is None else ends - count
                for t in range(NT):
                    base = z_row(x) + at
                    pack[t, base:base + count, :] = ref[x, row:row + count, 128 * t:128 * t + 128]
    greet(near)

    def copies(dt, dg, device):
        def remote(src, dst, send, recv):
            return pltpu.make_async_remote_copy(src_ref=src, dst_ref=dst, send_sem=send, recv_sem=recv,
                                                device_id=device, device_id_type=pl.DeviceIdType.MESH)
        if dg == 0:
            made, at = [], 0
            spans = (5, 4, 4) if dt == 1 else (4, 4, 4)
            out = xlo if dt == 1 else xhi
            side = 0 if dt == 1 else 1
            for n, (ref, count) in enumerate(zip((tx, ty, tz), spans)):
                first = 16 - count if dt == 1 else 0
                made.append(remote(ref.at[pl.ds(first, count)], out.at[pl.ds(at, count)],
                                   x_send.at[side, n], x_recv.at[side, n]))
                at += count
            return made
        pack = up if dg == 1 else down
        n = slot_of(dt, dg)
        m = slot_of(-dt, -dg)
        if dt == 0:
            return [remote(pack, zlo if dg == 1 else zhi, z_send.at[n], z_recv.at[m])]
        first = ZROWS - 56 if dt == 1 else 0
        corner = (0 if dt == 1 else 2) + (0 if dg == 1 else 1)
        return [remote(pack.at[:, pl.ds(first, 56), :], corners.at[corner], z_send.at[n], z_recv.at[m])]

    for dt, dg, here, device in sorted(near, key=lambda v: abs(v[0]) + abs(v[1])):
        @pl.when(here)
        def _():
            for copy in copies(dt, dg, device):
                copy.start()
    for dt, dg, here, device in near:
        @pl.when(here)
        def _():
            for copy in copies(-dt, -dg, device):
                copy.wait_recv()
            for copy in copies(dt, dg, device):
                copy.wait_send()


def run_halo(tx, ty, tz):
    shapes = ((13, 16, 512), (12, 16, 512), (NT, ZROWS, 128), (NT, ZROWS, 128), (4, NT, 56, 128))
    return pl.pallas_call(
        halo_kernel,
        name="halo",
        out_shape=tuple(jax.ShapeDtypeStruct(shape, F32) for shape in shapes),
        in_specs=[VMEM_SPEC] * 3,
        out_specs=(VMEM_SPEC,) * 5,
        scratch_shapes=[
            pltpu.VMEM((NT, ZROWS, 128), F32), pltpu.VMEM((NT, ZROWS, 128), F32),
            pltpu.SemaphoreType.DMA((2, 3)), pltpu.SemaphoreType.DMA((2, 3)),
            pltpu.SemaphoreType.DMA((9,)), pltpu.SemaphoreType.DMA((9,)),
        ],
        compiler_params=pltpu.CompilerParams(collective_id=0, has_side_effects=True),
        interpret=COMM_INTERPRET,
    )(tx, ty, tz)


def body(trans_x, trans_y, trans_z, accumulation, source, well_cell, well_rate):
    halos = run_halo(trans_x, trans_y, trans_z)
    basis, packed, rhs, xh, zh = run_main(trans_x, trans_y, trans_z, halos, accumulation, source, well_cell, well_rate)
    c4 = run_coarse(packed)
    pressure, residual = run_finish(trans_x, trans_y, trans_z, halos[0], halos[2], basis, xh, zh, c4, accumulation, rhs)
    return basis, pressure, residual


def solution(mesh):
    grid = P("tile", "gz", None)
    return jax.shard_map(
        body,
        mesh=mesh,
        in_specs=(grid,) * 5 + (P("tile", "gz"),) * 2,
        out_specs=(P(None, "tile", "gz", None), grid, grid),
        check_vma=False,
    )
```

```python
import jax
import jax.numpy as jnp
from jax import lax
from jax.experimental import pallas as pl
from jax.experimental.pallas import tpu as pltpu
from jax.sharding import PartitionSpec as P

COARSE_STEP = 0.5
NT = 4
NXE = 24
NR = 32
F32 = jnp.float32
INTERPRET = False
COMM_INTERPRET = False


def iota(shape, dim):
    return lax.broadcasted_iota(jnp.int32, shape, dim)


def roll(value, shift):
    return pltpu.roll(value, shift, 1)


def select_dot(table, value):
    total = None
    for _ in range(3):
        part = value.astype(jnp.bfloat16)
        value = value - part.astype(F32)
        term = jnp.dot(*table(part), preferred_element_type=F32)
        total = term if total is None else total + term
    return total


LO_SPANS = (4, 4, 5)
HI_SPANS = (4, 4, 4)
ZROWS = 216
CORNER_ROWS = (0, 0, 12, 21, 27)


def z_row(x):
    return 13 * x + 4 * (x >= 4)


def main_kernel(tx_in, ty_in, tz_in, xlo, xhi, zlo, zhi, corners, acc, src, wcell, wrate,
                basis_out, coarse_out, rhs_out, xh_out, zh_out,
                tx_s, ty_s, tz_s, tym_s, dd_s, b0, b1, sums, sem_in, sem_out, sem_x):
    loads = []
    pieces = ((tx_in, 0, 16, tx_s, 5), (xlo, 0, 5, tx_s, 0), (xhi, 0, 4, tx_s, 21),
              (ty_in, 0, 16, ty_s, 4), (xlo, 5, 4, ty_s, 0), (xhi, 4, 4, ty_s, 20),
              (tz_in, 0, 16, tz_s, 4), (xlo, 9, 4, tz_s, 0), (xhi, 8, 4, tz_s, 20))
    for t in range(NT):
        for k, (hbm, first_in, count, vmem, first_out) in enumerate(pieces):
            copy = pltpu.make_async_copy(hbm.at[pl.ds(first_in, count), :, pl.ds(128 * t, 128)],
                                         vmem.at[pl.ds(first_out, count), t, pl.ds(8, 16), :],
                                         sem_in.at[k * NT + t])
            copy.start()
            loads.append(copy)
    for x in range(-4, 20):
        for side, top, spans in ((0, 4, LO_SPANS), (1, 24, HI_SPANS)):
            for t in range(NT):
                for f, (ref, shift) in enumerate(((tx_s, 5), (ty_s, 4), (tz_s, 4))):
                    if 0 <= x < 16:
                        count = spans[f]
                        row = top - (count - 4)
                        base = z_row(x) + 4 * f
                        ref[x + shift, t, row:row + count, :] = (zlo, zhi)[side][t, base:base + count, :]
                    else:
                        layer = -x if x < 0 else x - 15
                        count = 5 - layer
                        row = top if side else 8 - count
                        base = CORNER_ROWS[layer] + f * count
                        ref[x + shift, t, row:row + count, :] = corners[2 * (x >= 16) + side, t, base:base + count, :]
    rhs_out[...] = src[...]
    lane_y = iota((1, 512), 1)
    for w in range(16):
        cell = wcell[0, w]
        row = cell // 512
        x, z, y = row // 16, row % 16, cell % 512
        old = rhs_out[x, pl.ds(z, 1), :]
        rhs_out[x, pl.ds(z, 1), :] = old + jnp.where(lane_y == y, wrate[0, w], 0.0)
    for copy in loads:
        copy.wait()

    @pl.when(lax.axis_index("tile") == lax.axis_size("tile") - 1)
    def _():
        for t in range(NT):
            tx_s[20, t, 0:32, :] = jnp.zeros((NR, 128), F32)

    @pl.when(lax.axis_index("gz") == lax.axis_size("gz") - 1)
    def _():
        for X in range(NXE):
            for t in range(NT):
                tz_s[X, t, 23:24, :] = jnp.zeros((1, 128), F32)

    sub = iota((8, 128), 0)
    lane = iota((8, 128), 1)
    yo = lane % 8
    lane_par = (lane // 8) % 2
    zero = jnp.zeros((8, 128), F32)

    def to_prev(value, left):
        return roll(jnp.where(lane == 127, left, value), 1)

    def to_next(value, right):
        return roll(jnp.where(lane == 0, right, value), 127)

    def distance(X):
        xo = (X + 4) % 8
        return jnp.where(xo < 4, xo + 1, 8 - xo)

    def first(X, carry):
        dist = distance(X)
        for kind, here in ((1, dist == 1), (2, (dist == 2) | (dist == 3)), (4, dist == 4)):
            @pl.when(here)
            def _():
                for t in range(NT):
                    first_tile(X, t, kind)
        return carry

    def first_tile(X, t, kind):
        tl = max(t - 1, 0)
        par = ((X + 4) // 8 + 1) % 2
        xo = (X + 4) % 8
        own_base, flip_base = par * 4, 4 - par * 4
        for r in range(3):
            R = 4 + 8 * r
            rows = pl.ds(R, 8)
            tx, txm = tx_s[X + 1, t, rows, :], tx_s[X, t, rows, :]
            tz, tzm = tz_s[X, t, rows, :], tz_s[X, t, pl.ds(R - 1, 8), :]
            ty = ty_s[X, t, rows, :]
            if t == NT - 1:
                ty = jnp.where(lane == 127, 0.0, ty)
                ty_s[X, t, rows, :] = ty
            tym = to_prev(ty, ty_s[X, tl, rows, :])
            if t == 0:
                tym = jnp.where(lane == 0, 0.0, tym)
            diag = tx + txm + tz + tzm + ty + tym
            half = diag * 0.5 + 1e-30
            tym_s[X, t, rows, :] = tym
            dd_s[X, t, rows, :] = half
            txb = jnp.where(xo == 0, txm, tx) if kind == 1 else zero
            tzb = jnp.where(sub == 3, tz, jnp.where(sub == 4, tzm, 0.0))
            tyb = jnp.where(yo == 7, ty, jnp.where(yo == 0, tym, 0.0))
            own = half + (diag - txb - tzb - tyb)
            inv = 1.0 / (own + txb + tzb + tyb)
            own, vx, vz, vy = own * inv, txb * inv, tzb * inv, tyb * inv
            row_par = jnp.where(sub < 4, (r + 1) % 2, r % 2)
            for c in range(2):
                for d in range(2):
                    in_row, in_lane = row_par == c, lane_par == d
                    value = jnp.where(in_row, jnp.where(in_lane, own, vy), jnp.where(in_lane, vz, 0.0))
                    b0[own_base + 2 * c + d, X, t, rows, :] = value
                    if kind == 1:
                        b0[flip_base + 2 * c + d, X, t, rows, :] = jnp.where(in_row & in_lane, vx, 0.0)
                    if kind == 4:
                        b1[flip_base + 2 * c + d, X, t, rows, :] = zero

    lax.fori_loop(0, NXE, first, 0)

    def sweep(old, new, k):
        def block(X, t, kind, par, up):
            n_slots = 4 if kind == 0 else 8
            tl, tr = max(t - 1, 0), min(t + 1, NT - 1)
            own_base, flip_base = par * 4, 4 - par * 4
            for r in range(3):
                R = 4 + 8 * r
                rows = pl.ds(R, 8)
                tx, txm = tx_s[X + 1, t, rows, :], tx_s[X, t, rows, :]
                tz, tzm = tz_s[X, t, rows, :], tz_s[X, t, pl.ds(R - 1, 8), :]
                ty, tym = ty_s[X, t, rows, :], tym_s[X, t, rows, :]
                half = dd_s[X, t, rows, :]
                row_par = jnp.where(sub < 4, (r + 1) % 2, r % 2)
                values = []
                for cd in range(n_slots):
                    c, d = (cd // 2) % 2, cd % 2
                    s = (own_base if cd < 4 else flip_base) + cd % 4
                    toward = tx_s[X + up, t, rows, :] * old[s, X - 1 + 2 * up, t, rows, :]
                    if cd >= 4 and kind == 1:
                        values.append(toward)
                        continue
                    b = old[s, X, t, rows, :]
                    v = half * b
                    if cd >= 4 and kind == 2:
                        v += toward
                    else:
                        v += tx * old[s, X + 1, t, rows, :]
                        v += txm * old[s, X - 1, t, rows, :]
                    v += tz * old[s, X, t, pl.ds(R + 1, 8), :]
                    v += tzm * old[s, X, t, pl.ds(R - 1, 8), :]
                    v += ty * to_next(b, old[s, X, tr, rows, :])
                    v += tym * to_prev(b, old[s, X, tl, rows, :])
                    if k == 4:
                        out_z = (row_par != c) & ((sub == 0) | (sub == 7))
                        out_y = (lane_par != d) & ((yo == 3) | (yo == 4))
                        v = jnp.where(out_z | out_y, 0.0, v)
                    values.append(v)
                total = values[0]
                for v in values[1:]:
                    total = total + v
                inv = 1.0 / total
                for cd in range(n_slots):
                    s = (own_base if cd < 4 else flip_base) + cd % 4
                    new[s, X, t, rows, :] = values[cd] * inv

        kinds = {}
        for away in range(1, 5):
            kind = 0 if away > min(k, 3) else 3 if away <= k - 2 else 2 if away == k - 1 else 1
            kinds.setdefault(kind, []).append(away)

        def step(X, carry):
            par = ((X + 4) // 8 + 1) % 2
            up = ((X + 4) % 8 >= 4).astype(jnp.int32)
            dist = distance(X)
            for kind, aways in kinds.items():
                @pl.when((dist >= aways[0]) & (dist <= aways[-1]))
                def _():
                    for t in range(NT):
                        block(X, t, kind, par, up)
            return carry

        lax.fori_loop(k - 1, 25 - k, step, 0)

    sweep(b0, b1, 2)
    sweep(b1, b0, 3)
    sweep(b0, b1, 4)

    stores = []
    for s in range(8):
        for t in range(NT):
            copy = pltpu.make_async_copy(b1.at[s, pl.ds(4, 16), t, pl.ds(8, 16), :],
                                         basis_out.at[s, :, :, pl.ds(128 * t, 128)], sem_out.at[s * NT + t])
            copy.start()
            stores.append(copy)
            for side, X in enumerate((3, 20)):
                copy = pltpu.make_async_copy(b1.at[s, X, t, pl.ds(8, 16), :],
                                             xh_out.at[s, side, :, pl.ds(128 * t, 128)],
                                             sem_x.at[(s * NT + t) * 2 + side])
                copy.start()
                stores.append(copy)

    flat = b1.reshape(8 * NXE * NT * NR, 128)

    def rows_of(index, carry):
        s, t = index // NT, index % NT
        lanes = pl.ds(pl.multiple_of(t * 128, 128), 128)
        for side, R in enumerate((7, 24)):
            for half in range(2):
                start = ((s * NXE + 4 + 8 * half) * NT + t) * NR + R
                zh_out[s, side, 8 * half:8 * half + 8, lanes] = flat[pl.ds(start, 8, stride=NT * NR), :]
        return carry

    lax.fori_loop(0, 8 * NT, rows_of, 0)

    for zb in range(2):
        R = 8 + 8 * zb

        def edges(index, carry):
            for n in range(2):
                edge_tile(index // 2, 2 * (index % 2) + n)
            return carry

        def edge_tile(xb, t):
            tl, tr = jnp.maximum(t - 1, 0), jnp.minimum(t + 1, NT - 1)
            rows = pl.ds(R, 8)
            lanes = pl.ds(pl.multiple_of(t * 128, 128), 128)
            own_base, flip_base = xb * 4, 4 - xb * 4
            groups = [[None] * 4 for _ in range(3)]
            scale = zero
            right = zero
            for xo in range(8):
                X = 4 + xb * 8 + xo
                x = xb * 8 + xo
                tz, tzm = tz_s[X, t, rows, :], tz_s[X, t, pl.ds(R - 1, 8), :]
                ty, tym = ty_s[X, t, rows, :], tym_s[X, t, rows, :]
                tzb = jnp.where(sub == 7, tz, jnp.where(sub == 0, tzm, 0.0))
                tyb = jnp.where(yo == 7, ty, jnp.where(yo == 0, tym, 0.0))
                central = acc[x, 8 * zb:8 * zb + 8, lanes] + tzb + tyb
                if xo == 0:
                    txb, xn = tx_s[X, t, rows, :], X - 1
                    central = central + txb
                if xo == 7:
                    txb, xn = tx_s[X + 1, t, rows, :], X + 1
                    central = central + txb
                scale = scale + central
                right = right + rhs_out[x, 8 * zb:8 * zb + 8, lanes]
                which = [(0, own_base)]
                if xo < 3:
                    which.append((1, flip_base))
                if xo > 4:
                    which.append((2, flip_base))
                for g, base in which:
                    for cd in range(4):
                        s = base + cd
                        b = b1[s, X, t, rows, :]
                        bz = jnp.where(sub == 7, b1[s, X, t, pl.ds(R + 1, 8), :], b1[s, X, t, pl.ds(R - 1, 8), :])
                        by = jnp.where(yo == 7, to_next(b, b1[s, X, tr, rows, :]), to_prev(b, b1[s, X, tl, rows, :]))
                        e = central * b - tzb * bz - tyb * by
                        if xo in (0, 7):
                            e = e - txb * b1[s, xn, t, rows, :]
                        groups[g][cd] = e if groups[g][cd] is None else groups[g][cd] + e
            for g in range(3):
                for cd in range(4):
                    u = xb * 12 + g * 4 + cd
                    sums[t, pl.ds(pl.multiple_of(u * 16 + 8 * zb, 8), 8), :] = groups[g][cd]
            sums[t, pl.ds(pl.multiple_of((24 + xb) * 16 + 8 * zb, 8), 8), :] = scale
            sums[t, pl.ds(pl.multiple_of((26 + xb) * 16 + 8 * zb, 8), 8), :] = right

        lax.fori_loop(0, 4, edges, 0)

    l_y, l_j = iota((128, 128), 0), iota((128, 128), 1)
    folded = jnp.zeros((448, 128), F32)
    for t in range(NT):
        target = ((l_y % 8) // 4) * 64 + 16 * t + l_y // 8
        chosen = (l_j == target).astype(jnp.bfloat16)
        folded = folded + select_dot(lambda part: (part, chosen), sums[t])
    o, i = iota((128, 448), 0), iota((128, 448), 1)
    pick = ((i // 16 == o % 32) & ((i % 16) // 4 == o // 32)).astype(jnp.bfloat16)
    quarters = select_dot(lambda part: (pick, part), folded)

    lane1 = iota((1, 128), 1)
    odd = lane1 % 2 == 1
    low = lane1 < 64

    def unit(q, u):
        return quarters[q * 32 + u:q * 32 + u + 1, :]

    def halves(value):
        return value + roll(value, 64)

    for xb in range(2):
        for dx, g in ((0, 1), (1, 0), (2, 2)):
            for dz in range(3):
                parts = []
                for zb in range(2):
                    c = zb if dz == 1 else 1 - zb
                    vs = []
                    for d in range(2):
                        u = xb * 12 + g * 4 + c * 2 + d
                        if dz == 0:
                            vs.append(unit(2 * zb, u))
                        elif dz == 2:
                            vs.append(unit(2 * zb + 1, u))
                        else:
                            vs.append(unit(2 * zb, u) + unit(2 * zb + 1, u))
                    own = jnp.where(odd, vs[1], vs[0])
                    flip = jnp.where(odd, vs[0], vs[1])
                    turned = roll(flip, 64)
                    parts.append((flip, halves(own), turned) if zb == 0 else (turned, halves(own), flip))
                for dy in range(3):
                    k = dx * 9 + dz * 3 + dy
                    coarse_out[xb, k:k + 1, :] = jnp.where(low, parts[0][dy], parts[1][dy])
        for k, u in ((27, 26 + xb), (28, 24 + xb)):
            parts = [halves(unit(2 * zb, u) + unit(2 * zb + 1, u)) for zb in range(2)]
            coarse_out[xb, k:k + 1, :] = jnp.where(low, parts[0], parts[1])
        coarse_out[xb, 29:32, :] = jnp.zeros((3, 128), F32)

    for copy in stores:
        copy.wait()


def finish_kernel(tx_in, ty_in, tz_in, xlo, zlo, basis, xh, zh, c4, acc, rhs, pressure_out, residual_out,
                  tx_s, ty_s, tz_s, g_s, p_s, sem_in):
    loads = []
    pieces = ((tx_in, 0, 16, tx_s, 1), (xlo, 4, 1, tx_s, 0), (ty_in, 0, 16, ty_s, 0), (tz_in, 0, 16, tz_s, 0))
    for t in range(NT):
        for k, (hbm, first_in, count, vmem, first_out) in enumerate(pieces):
            copy = pltpu.make_async_copy(hbm.at[pl.ds(first_in, count), :, pl.ds(128 * t, 128)],
                                         vmem.at[pl.ds(first_out, count), t, pl.ds(8, 16), :],
                                         sem_in.at[k * NT + t])
            copy.start()
            loads.append(copy)
        for x in range(16):
            tz_s[x, t, 7:8, :] = zlo[t, z_row(x) + 12:z_row(x) + 13, :]
    sub = iota((8, 128), 0)
    lane = iota((8, 128), 1)
    upper = sub >= 4

    j, y = iota((128, 512), 0), iota((128, 512), 1)
    block = y // 8
    side = jnp.where(y % 8 >= 4, 1, -1)
    spread = []
    for d in range(2):
        node = jnp.where(block % 2 == d, block, block + side)
        chosen = (j == node).astype(jnp.bfloat16)
        spread.append(select_dot(lambda part: (part, chosen), c4[...]))
    for nx in range(4):
        for c in range(2):
            for d in range(2):
                def row(nz):
                    return spread[d][nz * 8 + nx + 1:nz * 8 + nx + 2, :]
                if c == 0:
                    tiles = (row(1), row(1)), (row(1), row(3))
                else:
                    tiles = (row(0), row(2)), (row(2), row(2))
                for zb in range(2):
                    for t in range(NT):
                        a, b = (jnp.broadcast_to(v[:, 128 * t:128 * t + 128], (8, 128)) for v in tiles[zb])
                        g_s[nx, 2 * c + d, t, 8 * zb:8 * zb + 8, :] = jnp.where(upper, b, a)

    def plane_nodes(X):
        block_x = (X + 4) // 8 - 1
        par = (block_x + 2) % 2
        up = (X + 4) % 8 >= 4
        flip = block_x + 1 + jnp.where(up, 1, -1)
        own = block_x + 1
        return jnp.where(par == 0, own, flip), jnp.where(par == 0, flip, own)

    def prolong(read, X, t, zb):
        n0, n1 = plane_nodes(X)
        total = None
        for s in range(8):
            n = n0 if s < 4 else n1
            term = read(s) * g_s[n, s % 4, t, 8 * zb:8 * zb + 8, :]
            total = term if total is None else total + term
        return total

    def pressures(x, carry):
        for t in range(NT):
            lanes = pl.ds(t * 128, 128)
            for zb in range(2):
                p = prolong(lambda s: basis[s, x, 8 * zb:8 * zb + 8, lanes], x + 4, t, zb)
                p_s[x + 1, t, 8 + 8 * zb:16 + 8 * zb, :] = p
                pressure_out[x, 8 * zb:8 * zb + 8, lanes] = p
        return carry

    lax.fori_loop(0, 16, pressures, 0)

    def outer(t, carry):
        lanes = pl.ds(pl.multiple_of(t * 128, 128), 128)
        for zb in range(2):
            for s_x, X, at in ((0, 3, 0), (1, 20, 17)):
                p = prolong(lambda s: xh[s, s_x, 8 * zb:8 * zb + 8, lanes], X, t, zb)
                p_s[at, t, 8 + 8 * zb:16 + 8 * zb, :] = p
        return carry

    lax.fori_loop(0, NT, outer, 0)
    flat = p_s.reshape(18 * NT * NR, 128)
    for t in range(NT):
        cols = slice(128 * t, 128 * t + 128)
        for s_z, R in ((0, 7), (1, 24)):
            for half in range(2):
                total = None
                for s in range(8):
                    a, c, d = s // 4, (s // 2) % 2, s % 2
                    nz = (1, 0)[c] if s_z == 0 else (3, 2)[c]
                    def row(nx):
                        return jnp.broadcast_to(spread[d][nz * 8 + nx + 1:nz * 8 + nx + 2, cols], (8, 128))
                    if a == 0:
                        value = row(1) if half == 0 else jnp.where(upper, row(3), row(1))
                    else:
                        value = jnp.where(upper, row(2), row(0)) if half == 0 else row(2)
                    term = zh[s, s_z, 8 * half:8 * half + 8, cols] * value
                    total = term if total is None else total + term
                flat[pl.ds(((1 + 8 * half) * NT + t) * NR + R, 8, stride=NT * NR), :] = total
    for copy in loads:
        copy.wait()

    @pl.when(lax.axis_index("tile") == lax.axis_size("tile") - 1)
    def _():
        for t in range(NT):
            tx_s[16, t, 8:24, :] = jnp.zeros((16, 128), F32)

    @pl.when(lax.axis_index("gz") == lax.axis_size("gz") - 1)
    def _():
        for x in range(16):
            for t in range(NT):
                tz_s[x, t, 23:24, :] = jnp.zeros((1, 128), F32)

    def to_prev(value, left):
        return roll(jnp.where(lane == 127, left, value), 1)

    def to_next(value, right):
        return roll(jnp.where(lane == 0, right, value), 127)

    def residuals(x, carry):
        for t in range(NT):
            lanes = pl.ds(t * 128, 128)
            tl, tr = max(t - 1, 0), min(t + 1, NT - 1)
            for zb in range(2):
                R = 8 + 8 * zb
                rows = pl.ds(R, 8)
                p = p_s[x + 1, t, rows, :]
                ty = ty_s[x, t, rows, :]
                tym = to_prev(ty, ty_s[x, tl, rows, :])
                if t == 0:
                    tym = jnp.where(lane == 0, 0.0, tym)
                if t == NT - 1:
                    ty = jnp.where(lane == 127, 0.0, ty)
                flow = acc[x, 8 * zb:8 * zb + 8, lanes] * p
                flow += tx_s[x + 1, t, rows, :] * (p - p_s[x + 2, t, rows, :])
                flow += tx_s[x, t, rows, :] * (p - p_s[x, t, rows, :])
                flow += tz_s[x, t, rows, :] * (p - p_s[x + 1, t, pl.ds(R + 1, 8), :])
                flow += tz_s[x, t, pl.ds(R - 1, 8), :] * (p - p_s[x + 1, t, pl.ds(R - 1, 8), :])
                flow += ty * (p - to_next(p, p_s[x + 1, tr, rows, :]))
                flow += tym * (p - to_prev(p, p_s[x + 1, tl, rows, :]))
                residual_out[x, 8 * zb:8 * zb + 8, lanes] = rhs[x, 8 * zb:8 * zb + 8, lanes] - flow
        return carry

    lax.fori_loop(0, 16, residuals, 0)


VMEM_SPEC = pl.BlockSpec(memory_space=pltpu.VMEM)
SMEM_SPEC = pl.BlockSpec(memory_space=pltpu.SMEM)
ANY_SPEC = pl.BlockSpec(memory_space=pl.ANY)


def run_main(tx, ty, tz, halos, acc, src, wcell, wrate):
    field = pltpu.VMEM((NXE, NT, NR, 128), F32)
    return pl.pallas_call(
        main_kernel,
        name="sweeps",
        out_shape=(jax.ShapeDtypeStruct((8, 16, 16, 512), F32), jax.ShapeDtypeStruct((2, 32, 128), F32),
                   jax.ShapeDtypeStruct((16, 16, 512), F32), jax.ShapeDtypeStruct((8, 2, 16, 512), F32),
                   jax.ShapeDtypeStruct((8, 2, 16, 512), F32)),
        in_specs=[ANY_SPEC] * 5 + [VMEM_SPEC] * 5 + [SMEM_SPEC] * 2,
        out_specs=(ANY_SPEC, VMEM_SPEC, VMEM_SPEC, ANY_SPEC, VMEM_SPEC),
        scratch_shapes=[
            pltpu.VMEM((NXE + 1, NT, NR, 128), F32), field, field, field, field,
            pltpu.VMEM((8, NXE, NT, NR, 128), F32), pltpu.VMEM((8, NXE, NT, NR, 128), F32),
            pltpu.VMEM((NT, 448, 128), F32),
            pltpu.SemaphoreType.DMA((9 * NT,)), pltpu.SemaphoreType.DMA((8 * NT,)),
            pltpu.SemaphoreType.DMA((16 * NT,)),
        ],
        compiler_params=pltpu.CompilerParams(vmem_limit_bytes=60 * 1024 * 1024),
        interpret=INTERPRET,
    )(tx, ty, tz, *halos, acc, src, wcell, wrate)


def run_finish(tx, ty, tz, xlo, zlo, basis, xh, zh, c4, acc, rhs):
    return pl.pallas_call(
        finish_kernel,
        name="finish",
        out_shape=(jax.ShapeDtypeStruct((16, 16, 512), F32), jax.ShapeDtypeStruct((16, 16, 512), F32)),
        in_specs=[ANY_SPEC] * 4 + [VMEM_SPEC] * 7,
        out_specs=(VMEM_SPEC, VMEM_SPEC),
        scratch_shapes=[
            pltpu.VMEM((17, NT, 24, 128), F32), pltpu.VMEM((16, NT, 24, 128), F32), pltpu.VMEM((16, NT, 24, 128), F32),
            pltpu.VMEM((4, 4, NT, 16, 128), F32), pltpu.VMEM((18, NT, NR, 128), F32),
            pltpu.SemaphoreType.DMA((4 * NT,)),
        ],
        compiler_params=pltpu.CompilerParams(vmem_limit_bytes=60 * 1024 * 1024),
        interpret=INTERPRET,
    )(tx, ty, tz, xlo, zlo, basis, xh, zh, c4, acc, rhs)


NEAR = [(dt, dg) for dt in (-1, 0, 1) for dg in (-1, 0, 1) if (dt, dg) != (0, 0)]


def slot_of(dt, dg):
    return (dt + 1) * 3 + dg + 1


def neighbours():
    tile, gz = lax.axis_index("tile"), lax.axis_index("gz")
    tiles, layers = lax.axis_size("tile"), lax.axis_size("gz")
    found = []
    for dt, dg in NEAR:
        here = (tile + dt >= 0) & (tile + dt < tiles) & (gz + dg >= 0) & (gz + dg < layers)
        found.append((dt, dg, here, (tile + dt, gz + dg)))
    return found


def greet(near):
    barrier = pltpu.get_barrier_semaphore()
    count = 0
    for dt, dg, here, device in near:
        @pl.when(here)
        def _():
            pl.semaphore_signal(barrier, inc=1, device_id=device, device_id_type=pl.DeviceIdType.MESH)
        count = count + here.astype(jnp.int32)
    pl.semaphore_wait(barrier, count)


def coarse_kernel(packed, c_out, table, got, mine, op_send, op_recv, c_send, c_recv):
    near = neighbours()
    table[...] = jnp.zeros(table.shape, F32)
    got[...] = jnp.zeros(got.shape, F32)
    greet(near)

    def op_copies(dt, dg, device):
        made = []
        for n, xb in enumerate({1: (1,), -1: (0,), 0: (0, 1)}[dt]):
            made.append(pltpu.make_async_remote_copy(
                src_ref=packed.at[xb], dst_ref=table.at[pl.ds(((2 * (1 - dt) + xb) * 3 + 1 - dg) * 32, 32)],
                send_sem=op_send.at[slot_of(dt, dg), n], recv_sem=op_recv.at[slot_of(-dt, -dg), n],
                device_id=device, device_id_type=pl.DeviceIdType.MESH))
        return made

    def c_copy(r, dt, dg, device):
        return pltpu.make_async_remote_copy(
            src_ref=mine.at[r], dst_ref=got.at[r, slot_of(-dt, -dg)],
            send_sem=c_send.at[r, slot_of(dt, dg)], recv_sem=c_recv.at[r, slot_of(-dt, -dg)],
            device_id=device, device_id_type=pl.DeviceIdType.MESH)

    def each(act):
        for dt, dg, here, device in near:
            @pl.when(here)
            def _():
                act(dt, dg, device)

    def send(r):
        each(lambda dt, dg, device: c_copy(r, dt, dg, device).start())

    def arrive(r):
        each(lambda dt, dg, device: c_copy(r, -dt, -dg, device).wait_recv())

    for xb in range(2):
        mine[0, xb:xb + 1, :] = COARSE_STEP * packed[xb, 27:28, :] / packed[xb, 28:29, :]
        table[((2 + xb) * 3 + 1) * 32:((2 + xb) * 3 + 2) * 32, :] = packed[xb]
    send(0)
    each(lambda dt, dg, device: [c.start() for c in op_copies(dt, dg, device)])

    lane = iota((8, 128), 1)
    row = iota((8, 128), 0)

    def entry(g, k):
        return table[pl.ds(g * 32 + k, 8, stride=96), :]

    def gather(r):
        fields = []
        for g in range(3):
            parts = []
            for dt in (-1, 0, 1):
                parts.append(mine[r, 0:2, :] if (dt, g) == (0, 1) else got[r, slot_of(dt, g - 1), 0:2, :])
            fields.append(jnp.concatenate(parts + [jnp.zeros((2, 128), F32)], 0))
        return fields

    def lanes_from(fields, g, by):
        if by == 0:
            return fields[g]
        if by > 0:
            after = fields[min(g + 1, 2)]
            return jnp.where(lane < 128 - by, roll(fields[g], 128 - by), roll(after, 128 - by))
        before = fields[max(g - 1, 0)]
        return jnp.where(lane >= -by, roll(fields[g], -by), roll(before, -by))

    def iterate(fields):
        totals = [None] * 3
        for dx in (-1, 0, 1):
            moved = fields if dx == 0 else [pltpu.roll(f, 1 if dx == -1 else 7, 0) for f in fields]
            for dz in (-1, 0, 1):
                for dy in (-1, 0, 1):
                    k = (dx + 1) * 9 + (dz + 1) * 3 + dy + 1
                    for g in range(3):
                        term = entry(g, k) * lanes_from(moved, g, 64 * dz + dy)
                        totals[g] = term if totals[g] is None else totals[g] + term
        result = []
        for g in range(3):
            scale = entry(g, 28)
            safe = jnp.where(scale > 0.0, scale, 1.0)
            value = fields[g] + COARSE_STEP * (entry(g, 27) - totals[g]) / safe
            result.append(jnp.where(scale > 0.0, value, 0.0))
        return result

    arrive(0)
    each(lambda dt, dg, device: [c.wait_recv() for c in op_copies(-dt, -dg, device)])
    for r in range(3):
        if r:
            arrive(r)
        fields = iterate(gather(r))
        if r < 2:
            fields = iterate(fields)
            mine[r + 1, 0:2, :] = fields[1][2:4]
            send(r + 1)
    c_out[0:8, :] = roll(fields[0], 64)
    c_out[8:16, :] = fields[1]
    c_out[16:24, :] = roll(fields[1], 64)
    c_out[24:32, :] = fields[2]

    def drain(dt, dg, device):
        for copy in op_copies(dt, dg, device):
            copy.wait_send()
        for r in range(3):
            c_copy(r, dt, dg, device).wait_send()

    each(drain)


def run_coarse(packed):
    return pl.pallas_call(
        coarse_kernel,
        name="coarse",
        out_shape=jax.ShapeDtypeStruct((32, 128), F32),
        in_specs=[VMEM_SPEC],
        out_specs=VMEM_SPEC,
        scratch_shapes=[
            pltpu.VMEM((8 * 3 * 32, 128), F32), pltpu.VMEM((3, 9, 8, 128), F32), pltpu.VMEM((3, 8, 128), F32),
            pltpu.SemaphoreType.DMA((9, 2)), pltpu.SemaphoreType.DMA((9, 2)),
            pltpu.SemaphoreType.DMA((3, 9)), pltpu.SemaphoreType.DMA((3, 9)),
        ],
        compiler_params=pltpu.CompilerParams(collective_id=1, has_side_effects=True),
        interpret=COMM_INTERPRET,
    )(packed)


def halo_kernel(tx, ty, tz, xlo, xhi, zlo, zhi, corners, up, down, angles, x_send, x_recv, z_send, z_recv):
    near = neighbours()
    exists = {(dt, dg): here for dt, dg, here, _ in near}
    landing = {(-1, 0): xlo, (1, 0): xhi, (0, -1): zlo, (0, 1): zhi,
               (-1, -1): corners.at[0], (-1, 1): corners.at[1], (1, -1): corners.at[2], (1, 1): corners.at[3]}
    for where, ref in landing.items():
        @pl.when(jnp.logical_not(exists[where]))
        def _():
            ref[...] = jnp.zeros(ref.shape, F32)
    greet(near)

    def copies(dt, dg, device):
        def remote(src, dst, send, recv):
            return pltpu.make_async_remote_copy(src_ref=src, dst_ref=dst, send_sem=send, recv_sem=recv,
                                                device_id=device, device_id_type=pl.DeviceIdType.MESH)
        if dg == 0:
            made, at = [], 0
            spans = (5, 4, 4) if dt == 1 else (4, 4, 4)
            out = xlo if dt == 1 else xhi
            side = 0 if dt == 1 else 1
            for n, (ref, count) in enumerate(zip((tx, ty, tz), spans)):
                first = 16 - count if dt == 1 else 0
                made.append(remote(ref.at[pl.ds(first, count)], out.at[pl.ds(at, count)],
                                   x_send.at[side, n], x_recv.at[side, n]))
                at += count
            return made
        pack = up if dg == 1 else down
        n = slot_of(dt, dg)
        m = slot_of(-dt, -dg)
        if dt == 0:
            return [remote(pack, zlo if dg == 1 else zhi, z_send.at[n], z_recv.at[m])]
        corner = (0 if dt == 1 else 2) + (0 if dg == 1 else 1)
        return [remote(angles.at[corner], corners.at[corner], z_send.at[n], z_recv.at[m])]

    def start(chosen):
        for dt, dg, here, device in near:
            if chosen(dt, dg):
                @pl.when(here)
                def _():
                    for copy in copies(dt, dg, device):
                        copy.start()

    start(lambda dt, dg: dg == 0)
    for pack, spans, step in ((up, LO_SPANS, 1), (down, HI_SPANS, -1)):
        for x in range(16):
            for f, ref in enumerate((tx, ty, tz)):
                row = 16 - spans[f] if step == 1 else 0
                base = z_row(x) + 4 * f
                for t in range(NT):
                    pack[t, base:base + spans[f], :] = ref[x, row:row + spans[f], 128 * t:128 * t + 128]
        start(lambda dt, dg: dt == 0 and dg == step)
    for dt in (1, -1):
        for dg in (1, -1):
            corner = (0 if dt == 1 else 2) + (0 if dg == 1 else 1)
            for layer in range(1, 5):
                x, count = (16 - layer if dt == 1 else layer - 1), 5 - layer
                row = 16 - count if dg == 1 else 0
                for f, ref in enumerate((tx, ty, tz)):
                    base = CORNER_ROWS[layer] + f * count
                    for t in range(NT):
                        angles[corner, t, base:base + count, :] = ref[x, row:row + count, 128 * t:128 * t + 128]
    start(lambda dt, dg: dt != 0 and dg != 0)
    for dt, dg, here, device in near:
        @pl.when(here)
        def _():
            for copy in copies(-dt, -dg, device):
                copy.wait_recv()
            for copy in copies(dt, dg, device):
                copy.wait_send()


def run_halo(tx, ty, tz):
    shapes = ((13, 16, 512), (12, 16, 512), (NT, ZROWS, 128), (NT, ZROWS, 128), (4, NT, 32, 128))
    return pl.pallas_call(
        halo_kernel,
        name="halo",
        out_shape=tuple(jax.ShapeDtypeStruct(shape, F32) for shape in shapes),
        in_specs=[VMEM_SPEC] * 3,
        out_specs=(VMEM_SPEC,) * 5,
        scratch_shapes=[
            pltpu.VMEM((NT, ZROWS, 128), F32), pltpu.VMEM((NT, ZROWS, 128), F32), pltpu.VMEM((4, NT, 32, 128), F32),
            pltpu.SemaphoreType.DMA((2, 3)), pltpu.SemaphoreType.DMA((2, 3)),
            pltpu.SemaphoreType.DMA((9,)), pltpu.SemaphoreType.DMA((9,)),
        ],
        compiler_params=pltpu.CompilerParams(collective_id=0, has_side_effects=True),
        interpret=COMM_INTERPRET,
    )(tx, ty, tz)


def body(trans_x, trans_y, trans_z, accumulation, source, well_cell, well_rate):
    halos = run_halo(trans_x, trans_y, trans_z)
    basis, packed, rhs, xh, zh = run_main(trans_x, trans_y, trans_z, halos, accumulation, source,
                                            well_cell.reshape(1, 16), well_rate.reshape(1, 16))
    c4 = run_coarse(packed)
    pressure, residual = run_finish(trans_x, trans_y, trans_z, halos[0], halos[2], basis, xh, zh, c4, accumulation, rhs)
    return basis, pressure, residual


def solution(mesh):
    grid = P("tile", "gz", None)
    return jax.shard_map(
        body,
        mesh=mesh,
        in_specs=(grid,) * 5 + (P("tile", "gz"),) * 2,
        out_specs=(P(None, "tile", "gz", None), grid, grid),
        check_vma=False,
    )
```

```python
import jax
import jax.numpy as jnp
from jax import lax
from jax.experimental import pallas as pl
from jax.experimental.pallas import tpu as pltpu
from jax.sharding import PartitionSpec as P

COARSE_STEP = 0.5
NT = 4
NXE = 24
NR = 32
F32 = jnp.float32
INTERPRET = False
COMM_INTERPRET = False


def iota(shape, dim):
    return lax.broadcasted_iota(jnp.int32, shape, dim)


def roll(value, shift):
    return pltpu.roll(value, shift, 1)


def select_dot(table, value):
    total = None
    for _ in range(3):
        part = value.astype(jnp.bfloat16)
        value = value - part.astype(F32)
        term = jnp.dot(*table(part), preferred_element_type=F32)
        total = term if total is None else total + term
    return total


LO_SPANS = (4, 4, 5)
HI_SPANS = (4, 4, 4)
ZROWS = 216
CORNER_ROWS = (0, 0, 12, 21, 27)


def z_row(x):
    return 13 * x + 4 * (x >= 4)


def main_kernel(tx_in, ty_in, tz_in, xlo, xhi, zlo, zhi, corners, acc_in, src_in, wcell, wrate,
                basis_out, coarse_out, rhs_out, xh_out, zh_out,
                tx_s, ty_s, tz_s, tym_s, dd_s, b0, b1, sums, acc, sem_in, sem_out, sem_x):
    loads = []
    pieces = ((tx_in, 0, 16, tx_s, 5), (xlo, 0, 5, tx_s, 0), (xhi, 0, 4, tx_s, 21),
              (ty_in, 0, 16, ty_s, 4), (xlo, 5, 4, ty_s, 0), (xhi, 4, 4, ty_s, 20),
              (tz_in, 0, 16, tz_s, 4), (xlo, 9, 4, tz_s, 0), (xhi, 8, 4, tz_s, 20))
    for t in range(NT):
        for k, (hbm, first_in, count, vmem, first_out) in enumerate(pieces):
            copy = pltpu.make_async_copy(hbm.at[pl.ds(first_in, count), :, pl.ds(128 * t, 128)],
                                         vmem.at[pl.ds(first_out, count), t, pl.ds(8, 16), :],
                                         sem_in.at[k * NT + t])
            copy.start()
            loads.append(copy)
    fields = [pltpu.make_async_copy(hbm, vmem, sem_in.at[9 * NT + n])
              for n, (hbm, vmem) in enumerate(((src_in, rhs_out), (acc_in, acc)))]
    for copy in fields:
        copy.start()
    for x in range(-4, 20):
        for side, top, spans in ((0, 4, LO_SPANS), (1, 24, HI_SPANS)):
            for t in range(NT):
                for f, (ref, shift) in enumerate(((tx_s, 5), (ty_s, 4), (tz_s, 4))):
                    if 0 <= x < 16:
                        count = spans[f]
                        row = top - (count - 4)
                        base = z_row(x) + 4 * f
                        ref[x + shift, t, row:row + count, :] = (zlo, zhi)[side][t, base:base + count, :]
                    else:
                        layer = -x if x < 0 else x - 15
                        count = 5 - layer
                        row = top if side else 8 - count
                        base = CORNER_ROWS[layer] + f * count
                        ref[x + shift, t, row:row + count, :] = corners[2 * (x >= 16) + side, t, base:base + count, :]
    for copy in loads:
        copy.wait()

    @pl.when(lax.axis_index("tile") == lax.axis_size("tile") - 1)
    def _():
        for t in range(NT):
            tx_s[20, t, 0:32, :] = jnp.zeros((NR, 128), F32)

    @pl.when(lax.axis_index("gz") == lax.axis_size("gz") - 1)
    def _():
        for X in range(NXE):
            for t in range(NT):
                tz_s[X, t, 23:24, :] = jnp.zeros((1, 128), F32)

    sub = iota((8, 128), 0)
    lane = iota((8, 128), 1)
    yo = lane % 8
    lane_par = (lane // 8) % 2
    zero = jnp.zeros((8, 128), F32)

    def to_prev(value, left):
        return roll(jnp.where(lane == 127, left, value), 1)

    def to_next(value, right):
        return roll(jnp.where(lane == 0, right, value), 127)

    def distance(X):
        xo = (X + 4) % 8
        return jnp.where(xo < 4, xo + 1, 8 - xo)

    def first(X, carry):
        dist = distance(X)
        for kind, here in ((1, dist == 1), (2, (dist == 2) | (dist == 3)), (4, dist == 4)):
            @pl.when(here)
            def _():
                for t in range(NT):
                    first_tile(X, t, kind)
                    first_tile(NXE - 1 - X, t, kind)
        return carry

    def first_tile(X, t, kind):
        tl = max(t - 1, 0)
        par = ((X + 4) // 8 + 1) % 2
        xo = (X + 4) % 8
        own_base, flip_base = par * 4, 4 - par * 4
        for r in range(3):
            R = 4 + 8 * r
            rows = pl.ds(R, 8)
            tx, txm = tx_s[X + 1, t, rows, :], tx_s[X, t, rows, :]
            tz, tzm = tz_s[X, t, rows, :], tz_s[X, t, pl.ds(R - 1, 8), :]
            ty = ty_s[X, t, rows, :]
            if t == NT - 1:
                ty = jnp.where(lane == 127, 0.0, ty)
                ty_s[X, t, rows, :] = ty
            tym = to_prev(ty, ty_s[X, tl, rows, :])
            if t == 0:
                tym = jnp.where(lane == 0, 0.0, tym)
            diag = tx + txm + tz + tzm + ty + tym
            half = diag * 0.5 + 1e-30
            tym_s[X, t, rows, :] = tym
            dd_s[X, t, rows, :] = half
            txb = jnp.where(xo == 0, txm, tx) if kind == 1 else zero
            tzb = jnp.where(sub == 3, tz, jnp.where(sub == 4, tzm, 0.0))
            tyb = jnp.where(yo == 7, ty, jnp.where(yo == 0, tym, 0.0))
            own = half + (diag - txb - tzb - tyb)
            inv = 1.0 / (own + txb + tzb + tyb)
            own, vx, vz, vy = own * inv, txb * inv, tzb * inv, tyb * inv
            row_par = jnp.where(sub < 4, (r + 1) % 2, r % 2)
            for c in range(2):
                for d in range(2):
                    in_row, in_lane = row_par == c, lane_par == d
                    value = jnp.where(in_row, jnp.where(in_lane, own, vy), jnp.where(in_lane, vz, 0.0))
                    b0[own_base + 2 * c + d, X, t, rows, :] = value
                    if kind == 1:
                        b0[flip_base + 2 * c + d, X, t, rows, :] = jnp.where(in_row & in_lane, vx, 0.0)
                    if kind == 4:
                        b1[flip_base + 2 * c + d, X, t, rows, :] = zero

    lax.fori_loop(0, NXE // 2, first, 0)

    def sweep(old, new, k):
        def block(X, t, kind, par, up):
            n_slots = 4 if kind == 0 else 8
            tl, tr = max(t - 1, 0), min(t + 1, NT - 1)
            own_base, flip_base = par * 4, 4 - par * 4
            for r in range(3):
                R = 4 + 8 * r
                rows = pl.ds(R, 8)
                tx, txm = tx_s[X + 1, t, rows, :], tx_s[X, t, rows, :]
                tz, tzm = tz_s[X, t, rows, :], tz_s[X, t, pl.ds(R - 1, 8), :]
                ty, tym = ty_s[X, t, rows, :], tym_s[X, t, rows, :]
                half = dd_s[X, t, rows, :]
                row_par = jnp.where(sub < 4, (r + 1) % 2, r % 2)
                values = []
                for cd in range(n_slots):
                    c, d = (cd // 2) % 2, cd % 2
                    s = (own_base if cd < 4 else flip_base) + cd % 4
                    toward = tx_s[X + up, t, rows, :] * old[s, X - 1 + 2 * up, t, rows, :]
                    if cd >= 4 and kind == 1:
                        values.append(toward)
                        continue
                    b = old[s, X, t, rows, :]
                    v = half * b
                    if cd >= 4 and kind == 2:
                        v += toward
                    else:
                        v += tx * old[s, X + 1, t, rows, :]
                        v += txm * old[s, X - 1, t, rows, :]
                    v += tz * old[s, X, t, pl.ds(R + 1, 8), :]
                    v += tzm * old[s, X, t, pl.ds(R - 1, 8), :]
                    v += ty * to_next(b, old[s, X, tr, rows, :])
                    v += tym * to_prev(b, old[s, X, tl, rows, :])
                    if k == 4:
                        out_z = (row_par != c) & ((sub == 0) | (sub == 7))
                        out_y = (lane_par != d) & ((yo == 3) | (yo == 4))
                        v = jnp.where(out_z | out_y, 0.0, v)
                    values.append(v)
                total = values[0]
                for v in values[1:]:
                    total = total + v
                inv = 1.0 / total
                for cd in range(n_slots):
                    s = (own_base if cd < 4 else flip_base) + cd % 4
                    new[s, X, t, rows, :] = values[cd] * inv

        kinds = {}
        for away in range(1, 5):
            kind = 0 if away > min(k, 3) else 3 if away <= k - 2 else 2 if away == k - 1 else 1
            kinds.setdefault(kind, []).append(away)

        def step(X, carry):
            par = ((X + 4) // 8 + 1) % 2
            up = ((X + 4) % 8 >= 4).astype(jnp.int32)
            dist = distance(X)
            for kind, aways in kinds.items():
                @pl.when((dist >= aways[0]) & (dist <= aways[-1]))
                def _():
                    for t in range(NT):
                        block(X, t, kind, par, up)
                        block(NXE - 1 - X, t, kind, 1 - par, 1 - up)
            return carry

        lax.fori_loop(k - 1, NXE // 2, step, 0)

    sweep(b0, b1, 2)
    sweep(b1, b0, 3)
    sweep(b0, b1, 4)

    stores = []
    for s in range(8):
        for t in range(NT):
            copy = pltpu.make_async_copy(b1.at[s, pl.ds(4, 16), t, pl.ds(8, 16), :],
                                         basis_out.at[s, :, :, pl.ds(128 * t, 128)], sem_out.at[s * NT + t])
            copy.start()
            stores.append(copy)
            for side, X in enumerate((3, 20)):
                copy = pltpu.make_async_copy(b1.at[s, X, t, pl.ds(8, 16), :],
                                             xh_out.at[s, side, :, pl.ds(128 * t, 128)],
                                             sem_x.at[(s * NT + t) * 2 + side])
                copy.start()
                stores.append(copy)

    flat = b1.reshape(8 * NXE * NT * NR, 128)

    def rows_of(index, carry):
        s, t = index // NT, index % NT
        lanes = pl.ds(pl.multiple_of(t * 128, 128), 128)
        for side, R in enumerate((7, 24)):
            for half in range(2):
                start = ((s * NXE + 4 + 8 * half) * NT + t) * NR + R
                zh_out[s, side, 8 * half:8 * half + 8, lanes] = flat[pl.ds(start, 8, stride=NT * NR), :]
        return carry

    lax.fori_loop(0, 8 * NT, rows_of, 0)

    for copy in fields:
        copy.wait()
    lane_y = iota((1, 512), 1)
    for w in range(16):
        cell = wcell[0, w]
        row = cell // 512
        x, z, y = row // 16, row % 16, cell % 512
        old = rhs_out[x, pl.ds(z, 1), :]
        rhs_out[x, pl.ds(z, 1), :] = old + jnp.where(lane_y == y, wrate[0, w], 0.0)
    for zb in range(2):
        R = 8 + 8 * zb

        def edges(index, carry):
            for n in range(2):
                edge_tile(index // 2, 2 * (index % 2) + n)
            return carry

        def edge_tile(xb, t):
            tl, tr = jnp.maximum(t - 1, 0), jnp.minimum(t + 1, NT - 1)
            rows = pl.ds(R, 8)
            lanes = pl.ds(pl.multiple_of(t * 128, 128), 128)
            own_base, flip_base = xb * 4, 4 - xb * 4
            groups = [[None] * 4 for _ in range(3)]
            scale = zero
            right = zero
            for xo in range(8):
                X = 4 + xb * 8 + xo
                x = xb * 8 + xo
                tz, tzm = tz_s[X, t, rows, :], tz_s[X, t, pl.ds(R - 1, 8), :]
                ty, tym = ty_s[X, t, rows, :], tym_s[X, t, rows, :]
                tzb = jnp.where(sub == 7, tz, jnp.where(sub == 0, tzm, 0.0))
                tyb = jnp.where(yo == 7, ty, jnp.where(yo == 0, tym, 0.0))
                central = acc[x, 8 * zb:8 * zb + 8, lanes] + tzb + tyb
                if xo == 0:
                    txb, xn = tx_s[X, t, rows, :], X - 1
                    central = central + txb
                if xo == 7:
                    txb, xn = tx_s[X + 1, t, rows, :], X + 1
                    central = central + txb
                scale = scale + central
                right = right + rhs_out[x, 8 * zb:8 * zb + 8, lanes]
                which = [(0, own_base)]
                if xo < 3:
                    which.append((1, flip_base))
                if xo > 4:
                    which.append((2, flip_base))
                for g, base in which:
                    for cd in range(4):
                        s = base + cd
                        b = b1[s, X, t, rows, :]
                        bz = jnp.where(sub == 7, b1[s, X, t, pl.ds(R + 1, 8), :], b1[s, X, t, pl.ds(R - 1, 8), :])
                        by = jnp.where(yo == 7, to_next(b, b1[s, X, tr, rows, :]), to_prev(b, b1[s, X, tl, rows, :]))
                        e = central * b - tzb * bz - tyb * by
                        if xo in (0, 7):
                            e = e - txb * b1[s, xn, t, rows, :]
                        groups[g][cd] = e if groups[g][cd] is None else groups[g][cd] + e
            for g in range(3):
                for cd in range(4):
                    u = xb * 12 + g * 4 + cd
                    sums[t, pl.ds(pl.multiple_of(u * 16 + 8 * zb, 8), 8), :] = groups[g][cd]
            sums[t, pl.ds(pl.multiple_of((24 + xb) * 16 + 8 * zb, 8), 8), :] = scale
            sums[t, pl.ds(pl.multiple_of((26 + xb) * 16 + 8 * zb, 8), 8), :] = right

        lax.fori_loop(0, 4, edges, 0)

    l_y, l_j = iota((128, 128), 0), iota((128, 128), 1)
    folded = jnp.zeros((448, 128), F32)
    for t in range(NT):
        target = ((l_y % 8) // 4) * 64 + 16 * t + l_y // 8
        chosen = (l_j == target).astype(jnp.bfloat16)
        folded = folded + select_dot(lambda part: (part, chosen), sums[t])
    o, i = iota((128, 448), 0), iota((128, 448), 1)
    pick = ((i // 16 == o % 32) & ((i % 16) // 4 == o // 32)).astype(jnp.bfloat16)
    quarters = select_dot(lambda part: (pick, part), folded)

    lane1 = iota((1, 128), 1)
    odd = lane1 % 2 == 1
    low = lane1 < 64

    def unit(q, u):
        return quarters[q * 32 + u:q * 32 + u + 1, :]

    def halves(value):
        return value + roll(value, 64)

    for xb in range(2):
        for dx, g in ((0, 1), (1, 0), (2, 2)):
            for dz in range(3):
                parts = []
                for zb in range(2):
                    c = zb if dz == 1 else 1 - zb
                    vs = []
                    for d in range(2):
                        u = xb * 12 + g * 4 + c * 2 + d
                        if dz == 0:
                            vs.append(unit(2 * zb, u))
                        elif dz == 2:
                            vs.append(unit(2 * zb + 1, u))
                        else:
                            vs.append(unit(2 * zb, u) + unit(2 * zb + 1, u))
                    own = jnp.where(odd, vs[1], vs[0])
                    flip = jnp.where(odd, vs[0], vs[1])
                    turned = roll(flip, 64)
                    parts.append((flip, halves(own), turned) if zb == 0 else (turned, halves(own), flip))
                for dy in range(3):
                    k = dx * 9 + dz * 3 + dy
                    coarse_out[xb, k:k + 1, :] = jnp.where(low, parts[0][dy], parts[1][dy])
        for k, u in ((27, 26 + xb), (28, 24 + xb)):
            parts = [halves(unit(2 * zb, u) + unit(2 * zb + 1, u)) for zb in range(2)]
            coarse_out[xb, k:k + 1, :] = jnp.where(low, parts[0], parts[1])
        coarse_out[xb, 29:32, :] = jnp.zeros((3, 128), F32)

    for copy in stores:
        copy.wait()


def finish_kernel(tx_in, ty_in, tz_in, xlo, basis_in, xh_in, zh_in, acc_in, rhs_in, zlo, c4, pressure_out, residual_out,
                  tx_s, ty_s, tz_s, g_s, p_s, basis, xh, zh, acc, rhs, sem_in, sem_b):
    def plane(x):
        return pltpu.make_async_copy(basis_in.at[:, x], basis.at[:, x], sem_b.at[x])

    sides = [pltpu.make_async_copy(hbm, vmem, sem_b.at[16 + n])
             for n, (hbm, vmem) in enumerate(((xh_in, xh), (zh_in, zh)))]
    loads = [pltpu.make_async_copy(hbm, vmem, sem_b.at[18 + n])
             for n, (hbm, vmem) in enumerate(((acc_in, acc), (rhs_in, rhs)))]
    for x in range(16):
        plane(x).start()
    for copy in sides + loads:
        copy.start()
    pieces = ((tx_in, 0, 16, tx_s, 1), (xlo, 4, 1, tx_s, 0), (ty_in, 0, 16, ty_s, 0), (tz_in, 0, 16, tz_s, 0))
    for t in range(NT):
        for k, (hbm, first_in, count, vmem, first_out) in enumerate(pieces):
            copy = pltpu.make_async_copy(hbm.at[pl.ds(first_in, count), :, pl.ds(128 * t, 128)],
                                         vmem.at[pl.ds(first_out, count), t, pl.ds(8, 16), :],
                                         sem_in.at[k * NT + t])
            copy.start()
            loads.append(copy)
        for x in range(16):
            tz_s[x, t, 7:8, :] = zlo[t, z_row(x) + 12:z_row(x) + 13, :]
    sub = iota((8, 128), 0)
    lane = iota((8, 128), 1)
    upper = sub >= 4

    j, y = iota((128, 512), 0), iota((128, 512), 1)
    block = y // 8
    side = jnp.where(y % 8 >= 4, 1, -1)
    spread = []
    for d in range(2):
        node = jnp.where(block % 2 == d, block, block + side)
        chosen = (j == node).astype(jnp.bfloat16)
        spread.append(select_dot(lambda part: (part, chosen), c4[...]))
    for nx in range(4):
        for c in range(2):
            for d in range(2):
                def row(nz):
                    return spread[d][nz * 8 + nx + 1:nz * 8 + nx + 2, :]
                if c == 0:
                    tiles = (row(1), row(1)), (row(1), row(3))
                else:
                    tiles = (row(0), row(2)), (row(2), row(2))
                for zb in range(2):
                    for t in range(NT):
                        a, b = (jnp.broadcast_to(v[:, 128 * t:128 * t + 128], (8, 128)) for v in tiles[zb])
                        g_s[nx, 2 * c + d, t, 8 * zb:8 * zb + 8, :] = jnp.where(upper, b, a)

    def plane_nodes(X):
        block_x = (X + 4) // 8 - 1
        par = (block_x + 2) % 2
        up = (X + 4) % 8 >= 4
        flip = block_x + 1 + jnp.where(up, 1, -1)
        own = block_x + 1
        return jnp.where(par == 0, own, flip), jnp.where(par == 0, flip, own)

    def prolong(read, X, t, zb):
        n0, n1 = plane_nodes(X)
        total = None
        for s in range(8):
            n = n0 if s < 4 else n1
            term = read(s) * g_s[n, s % 4, t, 8 * zb:8 * zb + 8, :]
            total = term if total is None else total + term
        return total

    def pressures(x, carry):
        plane(x).wait()
        for t in range(NT):
            lanes = pl.ds(t * 128, 128)
            for zb in range(2):
                p = prolong(lambda s: basis[s, x, 8 * zb:8 * zb + 8, lanes], x + 4, t, zb)
                p_s[x + 1, t, 8 + 8 * zb:16 + 8 * zb, :] = p
                pressure_out[x, 8 * zb:8 * zb + 8, lanes] = p
        return carry

    lax.fori_loop(0, 16, pressures, 0)

    for copy in sides:
        copy.wait()

    def outer(t, carry):
        lanes = pl.ds(pl.multiple_of(t * 128, 128), 128)
        for zb in range(2):
            for s_x, X, at in ((0, 3, 0), (1, 20, 17)):
                p = prolong(lambda s: xh[s, s_x, 8 * zb:8 * zb + 8, lanes], X, t, zb)
                p_s[at, t, 8 + 8 * zb:16 + 8 * zb, :] = p
        return carry

    lax.fori_loop(0, NT, outer, 0)
    flat = p_s.reshape(18 * NT * NR, 128)
    for t in range(NT):
        cols = slice(128 * t, 128 * t + 128)
        for s_z, R in ((0, 7), (1, 24)):
            for half in range(2):
                total = None
                for s in range(8):
                    a, c, d = s // 4, (s // 2) % 2, s % 2
                    nz = (1, 0)[c] if s_z == 0 else (3, 2)[c]
                    def row(nx):
                        return jnp.broadcast_to(spread[d][nz * 8 + nx + 1:nz * 8 + nx + 2, cols], (8, 128))
                    if a == 0:
                        value = row(1) if half == 0 else jnp.where(upper, row(3), row(1))
                    else:
                        value = jnp.where(upper, row(2), row(0)) if half == 0 else row(2)
                    term = zh[s, s_z, 8 * half:8 * half + 8, cols] * value
                    total = term if total is None else total + term
                flat[pl.ds(((1 + 8 * half) * NT + t) * NR + R, 8, stride=NT * NR), :] = total
    for copy in loads:
        copy.wait()

    @pl.when(lax.axis_index("tile") == lax.axis_size("tile") - 1)
    def _():
        for t in range(NT):
            tx_s[16, t, 8:24, :] = jnp.zeros((16, 128), F32)

    @pl.when(lax.axis_index("gz") == lax.axis_size("gz") - 1)
    def _():
        for x in range(16):
            for t in range(NT):
                tz_s[x, t, 23:24, :] = jnp.zeros((1, 128), F32)

    def to_prev(value, left):
        return roll(jnp.where(lane == 127, left, value), 1)

    def to_next(value, right):
        return roll(jnp.where(lane == 0, right, value), 127)

    def residuals(x, carry):
        for t in range(NT):
            lanes = pl.ds(t * 128, 128)
            tl, tr = max(t - 1, 0), min(t + 1, NT - 1)
            for zb in range(2):
                R = 8 + 8 * zb
                rows = pl.ds(R, 8)
                p = p_s[x + 1, t, rows, :]
                ty = ty_s[x, t, rows, :]
                tym = to_prev(ty, ty_s[x, tl, rows, :])
                if t == 0:
                    tym = jnp.where(lane == 0, 0.0, tym)
                if t == NT - 1:
                    ty = jnp.where(lane == 127, 0.0, ty)
                flow = acc[x, 8 * zb:8 * zb + 8, lanes] * p
                flow += tx_s[x + 1, t, rows, :] * (p - p_s[x + 2, t, rows, :])
                flow += tx_s[x, t, rows, :] * (p - p_s[x, t, rows, :])
                flow += tz_s[x, t, rows, :] * (p - p_s[x + 1, t, pl.ds(R + 1, 8), :])
                flow += tz_s[x, t, pl.ds(R - 1, 8), :] * (p - p_s[x + 1, t, pl.ds(R - 1, 8), :])
                flow += ty * (p - to_next(p, p_s[x + 1, tr, rows, :]))
                flow += tym * (p - to_prev(p, p_s[x + 1, tl, rows, :]))
                residual_out[x, 8 * zb:8 * zb + 8, lanes] = rhs[x, 8 * zb:8 * zb + 8, lanes] - flow
        return carry

    lax.fori_loop(0, 16, residuals, 0)


VMEM_SPEC = pl.BlockSpec(memory_space=pltpu.VMEM)
SMEM_SPEC = pl.BlockSpec(memory_space=pltpu.SMEM)
ANY_SPEC = pl.BlockSpec(memory_space=pl.ANY)


def run_main(tx, ty, tz, halos, acc, src, wcell, wrate):
    field = pltpu.VMEM((NXE, NT, NR, 128), F32)
    return pl.pallas_call(
        main_kernel,
        name="sweeps",
        out_shape=(jax.ShapeDtypeStruct((8, 16, 16, 512), F32), jax.ShapeDtypeStruct((2, 32, 128), F32),
                   jax.ShapeDtypeStruct((16, 16, 512), F32), jax.ShapeDtypeStruct((8, 2, 16, 512), F32),
                   jax.ShapeDtypeStruct((8, 2, 16, 512), F32)),
        in_specs=[ANY_SPEC] * 5 + [VMEM_SPEC] * 3 + [ANY_SPEC] * 2 + [SMEM_SPEC] * 2,
        out_specs=(ANY_SPEC, VMEM_SPEC, VMEM_SPEC, ANY_SPEC, VMEM_SPEC),
        scratch_shapes=[
            pltpu.VMEM((NXE + 1, NT, NR, 128), F32), field, field, field, field,
            pltpu.VMEM((8, NXE, NT, NR, 128), F32), pltpu.VMEM((8, NXE, NT, NR, 128), F32),
            pltpu.VMEM((NT, 448, 128), F32), pltpu.VMEM((16, 16, 512), F32),
            pltpu.SemaphoreType.DMA((9 * NT + 2,)), pltpu.SemaphoreType.DMA((8 * NT,)),
            pltpu.SemaphoreType.DMA((16 * NT,)),
        ],
        compiler_params=pltpu.CompilerParams(vmem_limit_bytes=60 * 1024 * 1024),
        interpret=INTERPRET,
    )(tx, ty, tz, *halos, acc, src, wcell, wrate)


def run_finish(tx, ty, tz, xlo, zlo, basis, xh, zh, c4, acc, rhs):
    return pl.pallas_call(
        finish_kernel,
        name="finish",
        out_shape=(jax.ShapeDtypeStruct((16, 16, 512), F32), jax.ShapeDtypeStruct((16, 16, 512), F32)),
        in_specs=[ANY_SPEC] * 9 + [VMEM_SPEC] * 2,
        out_specs=(VMEM_SPEC, VMEM_SPEC),
        scratch_shapes=[
            pltpu.VMEM((17, NT, 24, 128), F32), pltpu.VMEM((16, NT, 24, 128), F32), pltpu.VMEM((16, NT, 24, 128), F32),
            pltpu.VMEM((4, 4, NT, 16, 128), F32), pltpu.VMEM((18, NT, NR, 128), F32),
            pltpu.VMEM((8, 16, 16, 512), F32), pltpu.VMEM((8, 2, 16, 512), F32), pltpu.VMEM((8, 2, 16, 512), F32),
            pltpu.VMEM((16, 16, 512), F32), pltpu.VMEM((16, 16, 512), F32),
            pltpu.SemaphoreType.DMA((4 * NT,)), pltpu.SemaphoreType.DMA((20,)),
        ],
        compiler_params=pltpu.CompilerParams(vmem_limit_bytes=60 * 1024 * 1024),
        interpret=INTERPRET,
    )(tx, ty, tz, xlo, basis, xh, zh, acc, rhs, zlo, c4)


NEAR = [(dt, dg) for dt in (-1, 0, 1) for dg in (-1, 0, 1) if (dt, dg) != (0, 0)]


def slot_of(dt, dg):
    return (dt + 1) * 3 + dg + 1


def neighbours():
    tile, gz = lax.axis_index("tile"), lax.axis_index("gz")
    tiles, layers = lax.axis_size("tile"), lax.axis_size("gz")
    found = []
    for dt, dg in NEAR:
        here = (tile + dt >= 0) & (tile + dt < tiles) & (gz + dg >= 0) & (gz + dg < layers)
        found.append((dt, dg, here, (tile + dt, gz + dg)))
    return found


def greet(near):
    barrier = pltpu.get_barrier_semaphore()
    count = 0
    for dt, dg, here, device in near:
        @pl.when(here)
        def _():
            pl.semaphore_signal(barrier, inc=1, device_id=device, device_id_type=pl.DeviceIdType.MESH)
        count = count + here.astype(jnp.int32)
    pl.semaphore_wait(barrier, count)


def coarse_kernel(packed, c_out, table, got, mine, op_send, op_recv, c_send, c_recv):
    near = neighbours()
    table[...] = jnp.zeros(table.shape, F32)
    got[...] = jnp.zeros(got.shape, F32)
    greet(near)

    def op_copies(dt, dg, device):
        made = []
        for n, xb in enumerate({1: (1,), -1: (0,), 0: (0, 1)}[dt]):
            made.append(pltpu.make_async_remote_copy(
                src_ref=packed.at[xb], dst_ref=table.at[pl.ds(((2 * (1 - dt) + xb) * 3 + 1 - dg) * 32, 32)],
                send_sem=op_send.at[slot_of(dt, dg), n], recv_sem=op_recv.at[slot_of(-dt, -dg), n],
                device_id=device, device_id_type=pl.DeviceIdType.MESH))
        return made

    def c_copy(r, dt, dg, device):
        return pltpu.make_async_remote_copy(
            src_ref=mine.at[r], dst_ref=got.at[r, slot_of(-dt, -dg)],
            send_sem=c_send.at[r, slot_of(dt, dg)], recv_sem=c_recv.at[r, slot_of(-dt, -dg)],
            device_id=device, device_id_type=pl.DeviceIdType.MESH)

    def each(act):
        for dt, dg, here, device in near:
            @pl.when(here)
            def _():
                act(dt, dg, device)

    def send(r):
        each(lambda dt, dg, device: c_copy(r, dt, dg, device).start())

    def arrive(r):
        each(lambda dt, dg, device: c_copy(r, -dt, -dg, device).wait_recv())

    for xb in range(2):
        mine[0, xb:xb + 1, :] = COARSE_STEP * packed[xb, 27:28, :] / packed[xb, 28:29, :]
        table[((2 + xb) * 3 + 1) * 32:((2 + xb) * 3 + 2) * 32, :] = packed[xb]
    send(0)
    each(lambda dt, dg, device: [c.start() for c in op_copies(dt, dg, device)])

    lane = iota((8, 128), 1)
    row = iota((8, 128), 0)

    def entry(g, k):
        return table[pl.ds(g * 32 + k, 8, stride=96), :]

    def gather(r):
        fields = []
        for g in range(3):
            parts = []
            for dt in (-1, 0, 1):
                parts.append(mine[r, 0:2, :] if (dt, g) == (0, 1) else got[r, slot_of(dt, g - 1), 0:2, :])
            fields.append(jnp.concatenate(parts + [jnp.zeros((2, 128), F32)], 0))
        return fields

    def lanes_from(fields, g, by):
        if by == 0:
            return fields[g]
        if by > 0:
            after = fields[min(g + 1, 2)]
            return jnp.where(lane < 128 - by, roll(fields[g], 128 - by), roll(after, 128 - by))
        before = fields[max(g - 1, 0)]
        return jnp.where(lane >= -by, roll(fields[g], -by), roll(before, -by))

    def iterate(fields):
        totals = [None] * 3
        for dx in (-1, 0, 1):
            moved = fields if dx == 0 else [pltpu.roll(f, 1 if dx == -1 else 7, 0) for f in fields]
            for dz in (-1, 0, 1):
                for dy in (-1, 0, 1):
                    k = (dx + 1) * 9 + (dz + 1) * 3 + dy + 1
                    for g in range(3):
                        term = entry(g, k) * lanes_from(moved, g, 64 * dz + dy)
                        totals[g] = term if totals[g] is None else totals[g] + term
        result = []
        for g in range(3):
            scale = entry(g, 28)
            safe = jnp.where(scale > 0.0, scale, 1.0)
            value = fields[g] + COARSE_STEP * (entry(g, 27) - totals[g]) / safe
            result.append(jnp.where(scale > 0.0, value, 0.0))
        return result

    arrive(0)
    each(lambda dt, dg, device: [c.wait_recv() for c in op_copies(-dt, -dg, device)])
    for r in range(3):
        if r:
            arrive(r)
        fields = iterate(gather(r))
        if r < 2:
            fields = iterate(fields)
            mine[r + 1, 0:2, :] = fields[1][2:4]
            send(r + 1)
    c_out[0:8, :] = roll(fields[0], 64)
    c_out[8:16, :] = fields[1]
    c_out[16:24, :] = roll(fields[1], 64)
    c_out[24:32, :] = fields[2]

    def drain(dt, dg, device):
        for copy in op_copies(dt, dg, device):
            copy.wait_send()
        for r in range(3):
            c_copy(r, dt, dg, device).wait_send()

    each(drain)


def run_coarse(packed):
    return pl.pallas_call(
        coarse_kernel,
        name="coarse",
        out_shape=jax.ShapeDtypeStruct((32, 128), F32),
        in_specs=[VMEM_SPEC],
        out_specs=VMEM_SPEC,
        scratch_shapes=[
            pltpu.VMEM((8 * 3 * 32, 128), F32), pltpu.VMEM((3, 9, 8, 128), F32), pltpu.VMEM((3, 8, 128), F32),
            pltpu.SemaphoreType.DMA((9, 2)), pltpu.SemaphoreType.DMA((9, 2)),
            pltpu.SemaphoreType.DMA((3, 9)), pltpu.SemaphoreType.DMA((3, 9)),
        ],
        compiler_params=pltpu.CompilerParams(collective_id=1, has_side_effects=True),
        interpret=COMM_INTERPRET,
    )(packed)


def halo_kernel(tx, ty, tz, xlo, xhi, zlo, zhi, corners, up, down, angles, x_send, x_recv, z_send, z_recv):
    near = neighbours()
    exists = {(dt, dg): here for dt, dg, here, _ in near}
    landing = {(-1, 0): xlo, (1, 0): xhi, (0, -1): zlo, (0, 1): zhi,
               (-1, -1): corners.at[0], (-1, 1): corners.at[1], (1, -1): corners.at[2], (1, 1): corners.at[3]}
    for where, ref in landing.items():
        @pl.when(jnp.logical_not(exists[where]))
        def _():
            ref[...] = jnp.zeros(ref.shape, F32)
    greet(near)

    def copies(dt, dg, device):
        def remote(src, dst, send, recv):
            return pltpu.make_async_remote_copy(src_ref=src, dst_ref=dst, send_sem=send, recv_sem=recv,
                                                device_id=device, device_id_type=pl.DeviceIdType.MESH)
        if dg == 0:
            made, at = [], 0
            spans = (5, 4, 4) if dt == 1 else (4, 4, 4)
            out = xlo if dt == 1 else xhi
            side = 0 if dt == 1 else 1
            for n, (ref, count) in enumerate(zip((tx, ty, tz), spans)):
                first = 16 - count if dt == 1 else 0
                made.append(remote(ref.at[pl.ds(first, count)], out.at[pl.ds(at, count)],
                                   x_send.at[side, n], x_recv.at[side, n]))
                at += count
            return made
        pack = up if dg == 1 else down
        n = slot_of(dt, dg)
        m = slot_of(-dt, -dg)
        if dt == 0:
            return [remote(pack, zlo if dg == 1 else zhi, z_send.at[n], z_recv.at[m])]
        corner = (0 if dt == 1 else 2) + (0 if dg == 1 else 1)
        return [remote(angles.at[corner], corners.at[corner], z_send.at[n], z_recv.at[m])]

    def start(chosen):
        for dt, dg, here, device in near:
            if chosen(dt, dg):
                @pl.when(here)
                def _():
                    for copy in copies(dt, dg, device):
                        copy.start()

    start(lambda dt, dg: dg == 0)
    for pack, spans, step in ((up, LO_SPANS, 1), (down, HI_SPANS, -1)):
        for x in range(16):
            for f, ref in enumerate((tx, ty, tz)):
                row = 16 - spans[f] if step == 1 else 0
                base = z_row(x) + 4 * f
                for t in range(NT):
                    pack[t, base:base + spans[f], :] = ref[x, row:row + spans[f], 128 * t:128 * t + 128]
        start(lambda dt, dg: dt == 0 and dg == step)
    for dt in (1, -1):
        for dg in (1, -1):
            corner = (0 if dt == 1 else 2) + (0 if dg == 1 else 1)
            for layer in range(1, 5):
                x, count = (16 - layer if dt == 1 else layer - 1), 5 - layer
                row = 16 - count if dg == 1 else 0
                for f, ref in enumerate((tx, ty, tz)):
                    base = CORNER_ROWS[layer] + f * count
                    for t in range(NT):
                        angles[corner, t, base:base + count, :] = ref[x, row:row + count, 128 * t:128 * t + 128]
    start(lambda dt, dg: dt != 0 and dg != 0)
    for dt, dg, here, device in near:
        @pl.when(here)
        def _():
            for copy in copies(-dt, -dg, device):
                copy.wait_recv()
            for copy in copies(dt, dg, device):
                copy.wait_send()


def run_halo(tx, ty, tz):
    shapes = ((13, 16, 512), (12, 16, 512), (NT, ZROWS, 128), (NT, ZROWS, 128), (4, NT, 32, 128))
    return pl.pallas_call(
        halo_kernel,
        name="halo",
        out_shape=tuple(jax.ShapeDtypeStruct(shape, F32) for shape in shapes),
        in_specs=[VMEM_SPEC] * 3,
        out_specs=(VMEM_SPEC,) * 5,
        scratch_shapes=[
            pltpu.VMEM((NT, ZROWS, 128), F32), pltpu.VMEM((NT, ZROWS, 128), F32), pltpu.VMEM((4, NT, 32, 128), F32),
            pltpu.SemaphoreType.DMA((2, 3)), pltpu.SemaphoreType.DMA((2, 3)),
            pltpu.SemaphoreType.DMA((9,)), pltpu.SemaphoreType.DMA((9,)),
        ],
        compiler_params=pltpu.CompilerParams(collective_id=0, has_side_effects=True),
        interpret=COMM_INTERPRET,
    )(tx, ty, tz)


def body(trans_x, trans_y, trans_z, accumulation, source, well_cell, well_rate):
    halos = run_halo(trans_x, trans_y, trans_z)
    basis, packed, rhs, xh, zh = run_main(trans_x, trans_y, trans_z, halos, accumulation, source,
                                            well_cell.reshape(1, 16), well_rate.reshape(1, 16))
    c4 = run_coarse(packed)
    pressure, residual = run_finish(trans_x, trans_y, trans_z, halos[0], halos[2], basis, xh, zh, c4, accumulation, rhs)
    return basis, pressure, residual


def solution(mesh):
    grid = P("tile", "gz", None)
    return jax.shard_map(
        body,
        mesh=mesh,
        in_specs=(grid,) * 5 + (P("tile", "gz"),) * 2,
        out_specs=(P(None, "tile", "gz", None), grid, grid),
        check_vma=False,
    )
```
